512 devices in a mesh: front: 2 (over core), row: 32 (over y, x), col: 8 (over z).
Axes of the slice: x: 4, y: 8, z: 8, core: 2. Of those that a mesh axis runs over, the one named last changes fastest.
Arguments:
- window: bfloat16 [2, 32768, 4096], P('front', 'row', 'col'), may hold values from -4 to 7.3, as said below
- children: bfloat16 [32768, 128, 128], P(('front', 'row', 'col')), may hold values from -4 to 4
- routes: int32 [32768, 1], P(('front', 'row', 'col')), may hold values from 0 to 63; in each aligned block of 64 rows (0 to 63, 64 to 127, ...) at most 2 rows name the same one
- slots: int32 [32768], P(('front', 'row', 'col')), may hold values from 0 to 15
- pattern: int32 [2, 64, 8], P('front', 'row', 'col'), may hold values 0 or 1
Outputs:
- factored: bfloat16 [2, 32768, 4096], P('front', 'row', 'col')
The draws below stay inside these ranges and needn't reach their ends.
Inputs may be any that keep to these rules, and one draw needn't show every extreme that they name: `routes`: among the rows of one device (aligned blocks of 64 rows) no owner group is named by more than 2 rows, a bound that some block reaches. `slots`: child blocks land only below the first tile row of each owner's part. `window`: each front's rows and columns [0, 512) hold a symmetric positive definite tile.
All inputs are finite; a program needn't handle non-finite values. No bound on the sum of `pattern` on one device may be relied on, other than what follows from the above.
Results may differ from the reference program's by a relative error of at most 0.0056.
Values may be sent and summed in bfloat16 or wider, within the bound.
No kernel may reach another device: no remote copies, remote signals or barrier semaphores. Data moves between devices by JAX's collectives and lax.ppermute only.
A program may use at most 64 MiB of HBM per device.

```python
import math
import jax
import jax.numpy as jnp
import numpy as np
from jax import lax

TILE = 512
SB = 128
TR_DEV = 2
CAP = 2
P_SIZE = 32768
NT = 64
CB = 64
SLOTS = 16
N_FRONT = 2
N_ROW = 32
N_COL = 8


def draw_window(key, part):
    keys = jax.random.split(key, 4)
    shape = (N_FRONT, P_SIZE, N_COL * TILE)
    base = jax.random.truncated_normal(keys[0], -4.0, 4.0, shape, jnp.float32)
    position = jnp.arange(TILE, dtype=jnp.float32)
    distance = jnp.abs(position[:, None] - position[None, :])
    gains = jax.random.uniform(keys[1], (N_FRONT, TILE), jnp.float32, 0.5, 1.5)
    noise = jax.random.uniform(keys[2], (N_FRONT, TILE, TILE), jnp.float32, -0.004, 0.004)
    noise = noise + jnp.swapaxes(noise, 1, 2)
    signs = jax.random.rademacher(keys[3], (N_FRONT, TILE, TILE), jnp.float32)
    upper_signs = jnp.triu(signs, 1)
    sign_term = 0.03 * (upper_signs + jnp.swapaxes(upper_signs, 1, 2))
    pivot = gains[:, :, None] * gains[:, None, :] * jnp.exp(-distance / 16.0)[None] + noise + sign_term + 4.9 * jnp.eye(TILE, dtype=jnp.float32)[None]
    base = base.at[:, :TILE, :TILE].set(pivot)
    return base.astype(jnp.bfloat16)


def touch_ends(drawn, stream_key, least, high):
    shape = drawn.shape
    index_at = [jax.random.randint(jax.random.fold_in(stream_key, axis), (), 0, shape[axis]) for axis in range(len(shape))]
    drawn = drawn.at[tuple(index_at)].set(least)
    longest = shape.index(max(shape))
    index_at[longest] = (index_at[longest] + 1) % shape[longest]
    return drawn.at[tuple(index_at)].set(high)


def level_of(own_key, shape, cuts, smallest, largest):
    def one(axis_at, shards_of):
        draws = jax.random.uniform(jax.random.fold_in(jax.random.fold_in(own_key, 6), axis_at), (shards_of,), jnp.float32, smallest / len(cuts), largest / len(cuts))
        return jnp.repeat(jnp.exp(draws), shape[axis_at] // shards_of).reshape((-1,) + (1,) * (len(shape) - axis_at - 1))

    loudness = one(*cuts[0])
    for cut in cuts[1:]:
        loudness = loudness * one(*cut)
    return loudness


def routed_block(key, own, number, rows, number_of, top, reach, skew):
    order = jax.random.permutation(key, number_of)
    crowded, usual = load_shares(number_of, rows * top, reach, skew, True), load_shares(number_of, rows * top, reach, skew, False)
    places = jnp.arange(number_of)

    def named(tallies, turn):
        used = int((tallies > 0).sum())
        fixed = max(1, used // 4)
        shifted = fixed + (places - fixed + turn * (used - fixed)) % max(1, number_of - fixed)
        return jnp.zeros((number_of,), jnp.int32).at[order[jnp.where(places < fixed, places, shifted)]].set(jnp.asarray(tallies, jnp.int32))

    tallies = jnp.where(number % 4 == 0, named(crowded, number // 4), named(usual, number - number // 4 - 1))
    mixed = jax.random.permutation(jax.random.fold_in(own, 3), number_of)
    giver, taker = mixed[0:number_of // 2 * 2:2], mixed[1:number_of // 2 * 2:2]
    margin = jnp.minimum(tallies[giver] - 1, reach - tallies[taker]) // 2
    margin = jnp.where((giver == order[0]) | (taker == order[0]) | (tallies[taker] == 0), 0, jnp.maximum(margin, 0))
    shifted = jax.random.randint(jax.random.fold_in(own, 4), (number_of // 2,), 0, 1 << 20) % (margin + 1)
    tallies = tallies.at[giver].add(-shifted).at[taker].add(shifted)
    labels = jnp.searchsorted(jnp.cumsum(tallies), jnp.arange(rows * top), side="right").astype(jnp.int32)
    table = labels.reshape(top, rows).T
    table = table[jax.random.permutation(jax.random.fold_in(own, 1), rows)]
    turn = jax.random.randint(jax.random.fold_in(own, 2), (rows, 1), 0, top)
    return jnp.take_along_axis(table, (jnp.arange(top)[None, :] + turn) % top, axis=1)


def load_shares(count, total, reach, skew, full):
    weights = [(1 << 20) // math.isqrt(grade ** skew) + 1 for grade in range(1, count + 1)]
    largest = reach if full else min(reach, max(-(-total // count), total * weights[0] // sum(weights)))
    least = 1 if total - largest >= count - 1 else 0
    holding, rest = [largest] + [least] * (count - 1), total - largest - least * (count - 1)
    while rest > 0:
        movable = [i for i in range(1, count) if holding[i] < largest] or [i for i in range(1, count) if holding[i] < reach]
        whole, remaining = sum([weights[i] for i in movable]), rest
        for i in movable:
            extra = min(reach - holding[i], max(1, remaining * weights[i] // whole), rest)
            holding[i] = holding[i] + extra
            rest = rest - extra
    return np.array(holding)


def scatter_about(rng, dims, width, limit, pieces=(), held_as=jnp.bfloat16):
    values = width * jax.random.normal(rng, dims, jnp.float32)
    if pieces:
        values = values * level_of(rng, dims, pieces, -0.22, 0.18)
    return jnp.clip(values, -limit, limit).astype(held_as)


def setup_inputs(seed: int = 0) -> dict:
    key_list = jax.random.split(jax.random.key(seed), 6)
    window = draw_window(jax.random.fold_in(key_list[5], 71), 0)
    children = scatter_about(key_list[1], (N_FRONT * N_ROW * N_COL * CB, SB, SB), 1.0, 4.0, ((0, 512),))
    routes_keys = jax.random.split(jax.random.fold_in(key_list[2], 1), (N_FRONT * N_ROW * N_COL * CB) // CB)
    routes_turns = jax.random.permutation(jax.random.fold_in(key_list[2], 3), (N_FRONT * N_ROW * N_COL * CB) // CB)
    routes = jax.vmap(lambda own, number: routed_block(jax.random.fold_in(key_list[2], 2), own, number, CB, N_FRONT * N_ROW, 1, CAP, 2))(routes_keys, routes_turns).reshape((N_FRONT * N_ROW * N_COL * CB, 1))
    slots = touch_ends(jax.random.randint(key_list[3], (N_FRONT * N_ROW * N_COL * CB,), 0, SLOTS), jax.random.fold_in(key_list[3], 1), 0, SLOTS - 1).astype(jnp.int32)
    pattern = touch_ends((jax.random.randint(key_list[4], (N_FRONT, NT, N_COL), 0, 3) < 2).astype(jnp.int32), jax.random.fold_in(key_list[4], 1), 0, 1)
    return dict(window=window, children=children, routes=routes, slots=slots, pattern=pattern)


def reference(window, children, routes, slots, pattern):
    side = TILE // SB
    row_blocks = P_SIZE // SB
    col_blocks = N_COL * side
    count = children.shape[0]
    owner_dev = jnp.arange(count, dtype=jnp.int32) // CB
    sender_col = owner_dev % N_COL
    target = routes[:, 0]
    target_front = target // N_ROW
    target_row = target % N_ROW
    block_row = target_row * (TR_DEV * side) + side + slots // side
    block_col = sender_col * side + slots % side

    def one_front(items):
        front_id, win, mask = items
        grid = win.astype(jnp.float32).reshape(row_blocks, SB, col_blocks, SB).transpose(0, 2, 1, 3)
        rows = jnp.where(target_front == front_id, block_row, row_blocks).astype(jnp.int32)
        grid = grid.at[rows, block_col].add(children.astype(jnp.float32), mode='drop')
        assembled = grid.transpose(0, 2, 1, 3).reshape(P_SIZE, N_COL * TILE)
        panel = assembled[:, :TILE]
        chol = jnp.linalg.cholesky(panel[:TILE])
        lower = jax.scipy.linalg.solve_triangular(chol, panel.T, lower=True).T.astype(jnp.bfloat16)
        lower_f = lower.astype(jnp.float32)
        update = jnp.dot(lower_f, lower_f[:N_COL * TILE].T, precision=lax.Precision.HIGHEST)
        live = jnp.repeat(jnp.repeat(mask.astype(jnp.float32), TILE, axis=0), TILE, axis=1)
        result = (assembled - live * update).astype(jnp.bfloat16)
        return result.at[:, :TILE].set(lower)
    fronts = jnp.arange(N_FRONT, dtype=jnp.int32)
    return lax.map(one_front, (fronts, window, pattern))
```

```python
import functools

import jax
import jax.numpy as jnp
from jax import lax
from jax.experimental import pallas as pl
from jax.experimental.pallas import tpu as pltpu
from jax.sharding import PartitionSpec as P

TILE = 512
SB = 128
CAP = 2
HI = lax.Precision.HIGHEST
F32 = jnp.float32
BF16 = jnp.bfloat16


def place_kernel(routes, slots, children, outgoing, tags, count, sem):
    n = children.shape[0]
    rows = tags.shape[0]

    def clear_tag(i, _):
        tags[i] = 0
        return 0

    lax.fori_loop(0, rows, clear_tag, 0)

    def clear_count(i, _):
        count[i] = 0
        return 0

    lax.fori_loop(0, count.shape[0], clear_count, 0)

    def send(k, _):
        g = routes[k]
        c = count[g]
        count[g] = c + 1
        at = g * CAP + c
        tags[at] = slots[k] + 1
        pltpu.make_async_copy(children.at[k], outgoing.at[at], sem).start()
        return 0

    lax.fori_loop(0, n, send, 0)
    pltpu.make_async_copy(children, outgoing.at[pl.ds(0, n)], sem).wait()


def place(routes, slots, children, groups):
    rows = groups * CAP
    smem = pl.BlockSpec(memory_space=pltpu.SMEM)
    return pl.pallas_call(
        place_kernel,
        out_shape=(
            jax.ShapeDtypeStruct((rows,) + children.shape[1:], children.dtype),
            jax.ShapeDtypeStruct((rows,), jnp.int32),
        ),
        in_specs=[smem, smem, pl.BlockSpec(memory_space=pl.ANY)],
        out_specs=(pl.BlockSpec(memory_space=pl.ANY), smem),
        scratch_shapes=[pltpu.SMEM((groups,), jnp.int32), pltpu.SemaphoreType.DMA],
        name="place",
    )(routes, slots, children)


def assemble_kernel(tags, incoming, base, out, acc):
    side = TILE // SB
    acc[...] = jnp.zeros_like(acc)

    def add(s, _):
        t = tags[s]

        @pl.when(t > 0)
        def _():
            acc[t - 1] = acc[t - 1] + incoming[s].astype(F32)

        return 0

    lax.fori_loop(0, incoming.shape[0], add, 0)
    for i in range(side):
        for j in range(side):
            rows, cols = slice(i * SB, (i + 1) * SB), slice(j * SB, (j + 1) * SB)
            out[rows, cols] = base[rows, cols].astype(F32) + acc[i * side + j]


def assemble(tags, incoming, base):
    vmem = pl.BlockSpec(memory_space=pltpu.VMEM)
    return pl.pallas_call(
        assemble_kernel,
        out_shape=jax.ShapeDtypeStruct((TILE, TILE), F32),
        in_specs=[pl.BlockSpec(memory_space=pltpu.SMEM), vmem, vmem],
        out_specs=vmem,
        scratch_shapes=[pltpu.VMEM(((TILE // SB) ** 2, SB, SB), F32)],
        compiler_params=pltpu.CompilerParams(vmem_limit_bytes=24 << 20),
        name="assemble",
    )(tags, incoming, base)


STEP = 4


def invert_block(block):
    n = block.shape[0]
    s = block
    row_at = lax.broadcasted_iota(jnp.int32, (n, n), 0)
    col_at = lax.broadcasted_iota(jnp.int32, (n, n), 1)
    w = jnp.where(row_at == col_at, 1.0, 0.0).astype(F32)
    done = []
    top = 0
    for j in range(0, n, STEP):
        local = j - top
        cols = [jnp.broadcast_to(s[:, j + a : j + a + 1], s.shape) for a in range(STEP)]
        r = [s[local + a : local + a + 1, :] for a in range(STEP)]
        v = [w[local + a : local + a + 1, :] for a in range(STEP)]
        p = [[cols[b][local + a : local + a + 1, :] for b in range(STEP)] for a in range(STEP)]
        inv = []
        m = [[None] * STEP for _ in range(STEP)]
        for b in range(STEP):
            inv.append(1.0 / p[b][b])
            for a in range(b + 1, STEP):
                m[a][b] = p[a][b] * inv[b]
                for c in range(b + 1, a + 1):
                    p[a][c] = p[a][c] - m[a][b] * p[c][b]
                r[a] = r[a] - m[a][b] * r[b]
                v[a] = v[a] - m[a][b] * v[b]
        done += [v[a] * lax.rsqrt(p[a][a]) for a in range(STEP)]
        if j + STEP >= n:
            break
        y = [None] * STEP
        z = [None] * STEP
        for a in reversed(range(STEP)):
            y[a] = r[a] * inv[a]
            z[a] = v[a] * inv[a]
            for b in range(a + 1, STEP):
                y[a] = y[a] - m[b][a] * y[b]
                z[a] = z[a] - m[b][a] * z[b]
        skip = (j + STEP) // 8 * 8 - top
        s, w = s[skip:], w[skip:]
        cols = [c[skip:] for c in cols]
        top += skip
        if top < j + STEP:
            keep = lax.broadcasted_iota(jnp.int32, s.shape, 0) >= j + STEP - top
            cols = [jnp.where(keep, c, 0.0) for c in cols]
        for a in range(STEP):
            s = s - cols[a] * y[a]
            w = w - cols[a] * z[a]
    return jnp.concatenate(done, axis=0)


def dot(a, b, dims):
    return lax.dot_general(a, b, (dims, ((), ())), precision=HI, preferred_element_type=F32)


def inverse_kernel(pivot, out, work, rest):
    n = pivot.shape[0]
    blocks = n // SB
    row_at = lax.broadcasted_iota(jnp.int32, (n, n), 0)
    col_at = lax.broadcasted_iota(jnp.int32, (n, n), 1)
    work[...] = pivot[...].astype(F32)
    rest[...] = jnp.where(row_at == col_at, 1.0, 0.0).astype(F32)

    def step(k, _):
        here = pl.ds(pl.multiple_of(k * SB, SB), SB)
        small = invert_block(work[here, here])
        panel = dot(work[:, here], small, ((1,), (1,)))
        below = lax.broadcasted_iota(jnp.int32, (n, SB), 0) >= (k + 1) * SB
        panel = jnp.where(below, panel, 0.0)
        work[...] = work[...] - dot(panel, panel, ((1,), (1,)))
        solved = dot(small, rest[here, :], ((1,), (0,)))
        out[here, :] = solved
        rest[...] = rest[...] - dot(panel, solved, ((1,), (0,)))
        return 0

    lax.fori_loop(0, blocks, step, 0)


def inverse_factor(pivot):
    n = pivot.shape[0]
    vmem = pl.BlockSpec(memory_space=pltpu.VMEM)
    return pl.pallas_call(
        inverse_kernel,
        out_shape=jax.ShapeDtypeStruct((n, n), F32),
        in_specs=[vmem],
        out_specs=vmem,
        scratch_shapes=[pltpu.VMEM((n, n), F32), pltpu.VMEM((n, n), F32)],
        compiler_params=pltpu.CompilerParams(vmem_limit_bytes=24 << 20),
        cost_estimate=pl.CostEstimate(flops=4 * n**3, bytes_accessed=6 * n * n, transcendentals=0),
        name="inverse",
    )(pivot)


def swap(block, axis):
    return lax.all_to_all(block, axis, split_axis=0, concat_axis=0, tiled=True)


def broadcast(block, axis, holder):
    parts = lax.axis_size(axis)
    rows, cols = block.shape
    got = swap(block.reshape(parts, rows // parts, cols), axis)
    mine = lax.dynamic_index_in_dim(got, holder, 0, keepdims=True)
    return swap(jnp.broadcast_to(mine, got.shape), axis).reshape(rows, cols)


def shards(window, children, routes, slots, pattern):
    groups = lax.axis_size("front") * lax.axis_size("row")
    column = lax.axis_index("col")
    first = window[0, :TILE]
    second = window[0, TILE:]
    pivot = broadcast(first, "row", 0)
    outgoing, marks = place(routes[:, 0], slots, children, groups)
    tags = swap(marks.reshape(groups, CAP), ("front", "row")).reshape(-1)
    incoming = swap(outgoing, ("front", "row"))
    inverse = inverse_factor(pivot)
    lower_first = lax.dot_general(
        first.astype(F32), inverse, (((1,), (1,)), ((), ())), precision=HI
    ).astype(BF16)
    added = assemble(tags, incoming, second)
    lower_second = lax.dot_general(
        added, inverse, (((1,), (1,)), ((), ())), precision=HI
    ).astype(BF16)
    lower_first = broadcast(lower_first, "col", 0)
    lower_second = broadcast(lower_second, "col", 0)
    owner = column // 2
    piece = jnp.where(column % 2 == 0, lower_first, lower_second)
    partner = broadcast(piece, "row", owner)

    def finish(lower, assembled, live):
        product = lax.dot_general(
            lower, partner, (((1,), (1,)), ((), ())), preferred_element_type=F32
        )
        updated = (assembled - live.astype(F32) * product).astype(BF16)
        return jnp.where(column == 0, lower, updated)

    return jnp.concatenate(
        [
            finish(lower_first, first.astype(F32), pattern[0, 0, 0]),
            finish(lower_second, added, pattern[0, 1, 0]),
        ],
        axis=0,
    )[None]


def solution(mesh):
    placed = (
        P("front", "row", "col"),
        P(("front", "row", "col"), None, None),
        P(("front", "row", "col"), None),
        P(("front", "row", "col")),
        P("front", "row", "col"),
    )
    return jax.shard_map(
        shards, mesh=mesh, in_specs=placed, out_specs=P("front", "row", "col"), check_vma=False
    )
```

```python
import functools

import jax
import jax.numpy as jnp
from jax import lax
from jax.experimental import pallas as pl
from jax.experimental.pallas import tpu as pltpu
from jax.sharding import PartitionSpec as P

TILE = 512
SB = 128
CAP = 2
HI = lax.Precision.HIGHEST
F32 = jnp.float32
BF16 = jnp.bfloat16


def place_kernel(routes, slots, children, outgoing, tags, count, sem):
    n = children.shape[0]
    rows = tags.shape[0]

    def clear_tag(i, _):
        tags[i] = 0
        return 0

    lax.fori_loop(0, rows, clear_tag, 0)

    def clear_count(i, _):
        count[i] = 0
        return 0

    lax.fori_loop(0, count.shape[0], clear_count, 0)

    def send(k, _):
        g = routes[k]
        c = count[g]
        count[g] = c + 1
        at = g * CAP + c
        tags[at] = slots[k] + 1
        pltpu.make_async_copy(children.at[k], outgoing.at[at], sem).start()
        return 0

    lax.fori_loop(0, n, send, 0)
    pltpu.make_async_copy(children, outgoing.at[pl.ds(0, n)], sem).wait()


def place(routes, slots, children, groups):
    rows = groups * CAP
    smem = pl.BlockSpec(memory_space=pltpu.SMEM)
    return pl.pallas_call(
        place_kernel,
        out_shape=(
            jax.ShapeDtypeStruct((rows,) + children.shape[1:], children.dtype),
            jax.ShapeDtypeStruct((rows,), jnp.int32),
        ),
        in_specs=[smem, smem, pl.BlockSpec(memory_space=pltpu.VMEM)],
        out_specs=(pl.BlockSpec(memory_space=pl.ANY), smem),
        scratch_shapes=[pltpu.SMEM((groups,), jnp.int32), pltpu.SemaphoreType.DMA],
        name="place",
    )(routes, slots, children)


def assemble_kernel(tags, incoming, base, out, acc):
    side = TILE // SB
    acc[...] = jnp.zeros_like(acc)

    def add(s, _):
        t = tags[s]

        @pl.when(t > 0)
        def _():
            acc[t - 1] = acc[t - 1] + incoming[s].astype(F32)

        return 0

    lax.fori_loop(0, incoming.shape[0], add, 0)
    for i in range(side):
        for j in range(side):
            rows, cols = slice(i * SB, (i + 1) * SB), slice(j * SB, (j + 1) * SB)
            out[rows, cols] = base[rows, cols].astype(F32) + acc[i * side + j]


def assemble(tags, incoming, base):
    vmem = pl.BlockSpec(memory_space=pltpu.VMEM)
    return pl.pallas_call(
        assemble_kernel,
        out_shape=jax.ShapeDtypeStruct((TILE, TILE), F32),
        in_specs=[pl.BlockSpec(memory_space=pltpu.SMEM), vmem, vmem],
        out_specs=vmem,
        scratch_shapes=[pltpu.VMEM(((TILE // SB) ** 2, SB, SB), F32)],
        compiler_params=pltpu.CompilerParams(vmem_limit_bytes=24 << 20),
        name="assemble",
    )(tags, incoming, base)


STEP = 4


def invert_block(block):
    n = block.shape[0]
    s = block
    row_at = lax.broadcasted_iota(jnp.int32, (n, n), 0)
    col_at = lax.broadcasted_iota(jnp.int32, (n, n), 1)
    w = jnp.where(row_at == col_at, 1.0, 0.0).astype(F32)
    done = []
    top = 0
    for j in range(0, n, STEP):
        local = j - top
        cols = [jnp.broadcast_to(s[:, j + a : j + a + 1], s.shape) for a in range(STEP)]
        r = [s[local + a : local + a + 1, :] for a in range(STEP)]
        v = [w[local + a : local + a + 1, :] for a in range(STEP)]
        p = [[cols[b][local + a : local + a + 1, :] for b in range(STEP)] for a in range(STEP)]
        inv = []
        m = [[None] * STEP for _ in range(STEP)]
        for b in range(STEP):
            inv.append(1.0 / p[b][b])
            for a in range(b + 1, STEP):
                m[a][b] = p[a][b] * inv[b]
                for c in range(b + 1, a + 1):
                    p[a][c] = p[a][c] - m[a][b] * p[c][b]
                r[a] = r[a] - m[a][b] * r[b]
                v[a] = v[a] - m[a][b] * v[b]
        done += [v[a] * lax.rsqrt(p[a][a]) for a in range(STEP)]
        if j + STEP >= n:
            break
        y = [None] * STEP
        z = [None] * STEP
        for a in reversed(range(STEP)):
            y[a] = r[a] * inv[a]
            z[a] = v[a] * inv[a]
            for b in range(a + 1, STEP):
                y[a] = y[a] - m[b][a] * y[b]
                z[a] = z[a] - m[b][a] * z[b]
        skip = (j + STEP) // 8 * 8 - top
        s, w = s[skip:], w[skip:]
        cols = [c[skip:] for c in cols]
        top += skip
        if top < j + STEP:
            keep = lax.broadcasted_iota(jnp.int32, s.shape, 0) >= j + STEP - top
            cols = [jnp.where(keep, c, 0.0) for c in cols]
        for a in range(STEP):
            s = s - cols[a] * y[a]
            w = w - cols[a] * z[a]
    return jnp.concatenate(done, axis=0)


def dot(a, b, dims):
    return lax.dot_general(a, b, (dims, ((), ())), precision=HI, preferred_element_type=F32)


def inverse_kernel(pivot, out, work, rest):
    n = pivot.shape[0]
    blocks = n // SB
    row_at = lax.broadcasted_iota(jnp.int32, (n, n), 0)
    col_at = lax.broadcasted_iota(jnp.int32, (n, n), 1)
    work[...] = pivot[...].astype(F32)
    rest[...] = jnp.where(row_at == col_at, 1.0, 0.0).astype(F32)

    def step(k, _):
        here = pl.ds(pl.multiple_of(k * SB, SB), SB)
        block = work[here, here]
        at = [lax.broadcasted_iota(jnp.int32, block.shape, d) for d in (0, 1)]
        small = invert_block(jnp.where(at[0] >= at[1], block, block.T))
        panel = dot(work[:, here], small, ((1,), (1,)))
        below = lax.broadcasted_iota(jnp.int32, (n, SB), 0) >= (k + 1) * SB
        panel = jnp.where(below, panel, 0.0)
        work[...] = work[...] - dot(panel, panel, ((1,), (1,)))
        solved = dot(small, rest[here, :], ((1,), (0,)))
        out[here, :] = solved
        rest[...] = rest[...] - dot(panel, solved, ((1,), (0,)))
        return 0

    lax.fori_loop(0, blocks, step, 0)


def inverse_factor(pivot):
    n = pivot.shape[0]
    vmem = pl.BlockSpec(memory_space=pltpu.VMEM)
    return pl.pallas_call(
        inverse_kernel,
        out_shape=jax.ShapeDtypeStruct((n, n), F32),
        in_specs=[vmem],
        out_specs=vmem,
        scratch_shapes=[pltpu.VMEM((n, n), F32), pltpu.VMEM((n, n), F32)],
        compiler_params=pltpu.CompilerParams(vmem_limit_bytes=24 << 20),
        cost_estimate=pl.CostEstimate(flops=4 * n**3, bytes_accessed=6 * n * n, transcendentals=0),
        name="inverse",
    )(pivot)


def swap(block, axis):
    return lax.all_to_all(block, axis, split_axis=0, concat_axis=0, tiled=True)


def circulate(part, axis):
    size = lax.axis_size(axis)
    parts = [part]
    for t in range(1, size):
        parts.append(lax.ppermute(part, axis, [(i, (i - t) % size) for i in range(size)]))
    return parts


def finish_kernel(size, state, *refs):
    parts = refs[:size]
    partner, base, added, out = refs[size:]
    column = state[0]
    rows = parts[0].shape[0] // 2
    for t in range(size):
        source = lax.rem(column + t, size)
        at = pl.ds(pl.multiple_of(source * rows, rows), rows)
        under = pl.ds(pl.multiple_of(source * rows + TILE, rows), rows)

        @pl.when(column == 0)
        def _():
            out[0, at, :] = parts[t][:rows, :]
            out[0, under, :] = parts[t][rows:, :]

        @pl.when(column != 0)
        def _():
            product = lax.dot_general(
                parts[t][...], partner[...], (((1,), (1,)), ((), ())), preferred_element_type=F32
            )
            upper = base[0, at, :].astype(F32) - state[1].astype(F32) * product[:rows]
            out[0, at, :] = upper.astype(BF16)
            lower = added[at, :] - state[2].astype(F32) * product[rows:]
            out[0, under, :] = lower.astype(BF16)


def finish(state, parts, partner, window, added):
    size = len(parts)
    vmem = pl.BlockSpec(memory_space=pltpu.VMEM)
    return pl.pallas_call(
        functools.partial(finish_kernel, size),
        out_shape=jax.ShapeDtypeStruct((1, 2 * TILE, TILE), BF16),
        grid=(1,),
        in_specs=[pl.BlockSpec(memory_space=pltpu.SMEM)]
        + [vmem] * (size + 1)
        + [pl.BlockSpec((1, TILE, TILE), lambda i: (0, 0, 0)), vmem],
        out_specs=vmem,
        compiler_params=pltpu.CompilerParams(vmem_limit_bytes=24 << 20),
        name="finish",
    )(state, *parts, partner, window, added)


def hand_out(parts, axis):
    mine = jnp.zeros_like(parts[-1] if parts[0] is None else parts[0])
    if parts[0] is not None:
        mine = jnp.where(lax.axis_index(axis) == 0, parts[0], mine)
    for p in range(1, len(parts)):
        if parts[p] is not None:
            mine = mine + lax.ppermute(parts[p], axis, [(0, p)])
    return mine


def shards(window, children, routes, slots, pattern):
    fronts = lax.axis_size("front")
    rows_axis = lax.axis_size("row")
    columns = lax.axis_size("col")
    front = lax.axis_index("front")
    column = lax.axis_index("col")
    first = window[0, :TILE]
    second = window[0, TILE:]
    part_rows = TILE // rows_axis
    marks_each = fronts * CAP
    even_raw = swap(first.reshape(rows_axis, part_rows, TILE), "row")[: columns // 2]
    outgoing, marks = place(routes[:, 0], slots, children, fronts * rows_axis)
    marks = marks.reshape(fronts, rows_axis, CAP)
    near = jnp.where(front == 0, marks[0], marks[1])
    far = jnp.where(front == 0, marks[1], marks[0])
    far = lax.ppermute(far, "front", [(0, 1), (1, 0)])
    both = jnp.concatenate([near, far], axis=1).astype(BF16)
    both = jnp.pad(both, ((0, 0), (TILE - marks_each, 0)))[:, None, :]
    place_row = lax.broadcasted_iota(jnp.int32, (rows_axis, part_rows, TILE), 1)
    place_col = lax.broadcasted_iota(jnp.int32, (rows_axis, part_rows, TILE), 2)
    spread = jnp.where(
        (place_row == 0) & (place_col >= TILE - marks_each), both, even_raw[0][None]
    )
    pivot = swap(spread, "row")
    got = pivot[:, 0, TILE - marks_each :].astype(jnp.int32).reshape(rows_axis, fronts, CAP)
    near, far = got[:, 0], got[:, 1]
    tags = jnp.stack([jnp.where(front == 0, near, far), jnp.where(front == 0, far, near)])
    tags = tags.reshape(-1)
    pivot = pivot.reshape(TILE, TILE)
    outgoing, tags, pivot = lax.optimization_barrier((outgoing, tags, pivot))
    incoming = swap(outgoing, ("front", "row"))
    inverse = inverse_factor(pivot)

    def solve(rows):
        return lax.dot_general(
            rows.astype(F32), inverse, (((1,), (1,)), ((), ())), precision=HI
        ).astype(BF16)

    def to_columns(lower):
        return hand_out(list(lower.reshape(columns, TILE // columns, TILE)), "col")

    even = solve(even_raw.reshape(-1, TILE)).reshape(even_raw.shape)
    even_part = hand_out(
        [even[c // 2] if c % 2 == 0 else None for c in range(columns)], "col"
    )
    first_part = to_columns(solve(first))
    incoming, even_part, first_part = lax.optimization_barrier((incoming, even_part, first_part))
    added = assemble(tags, incoming, second)
    lower_second = solve(added)
    odd = swap(lower_second.reshape(rows_axis, part_rows, TILE), "row")
    second_part = to_columns(lower_second)
    odd, second_part = lax.optimization_barrier((odd, second_part))
    odd_part = hand_out(
        [odd[c // 2] if c % 2 == 1 else None for c in range(columns)], "col"
    )
    lower = circulate(jnp.concatenate([first_part, second_part], axis=0), "col")
    partner_part = jnp.where(column % 2 == 0, even_part, odd_part)
    partner = swap(
        jnp.broadcast_to(partner_part[None], (rows_axis,) + partner_part.shape), "row"
    ).reshape(TILE, TILE)

    state = jnp.concatenate([jnp.full((1,), column, jnp.int32), pattern[0, :, 0]])
    return finish(state, lower, partner, window, added)


def solution(mesh):
    placed = (
        P("front", "row", "col"),
        P(("front", "row", "col"), None, None),
        P(("front", "row", "col"), None),
        P(("front", "row", "col")),
        P("front", "row", "col"),
    )
    return jax.shard_map(
        shards, mesh=mesh, in_specs=placed, out_specs=P("front", "row", "col"), check_vma=False
    )
```

```python
import functools

import jax
import jax.numpy as jnp
from jax import lax
from jax.experimental import pallas as pl
from jax.experimental.pallas import tpu as pltpu
from jax.sharding import PartitionSpec as P

TILE = 512
SB = 128
CAP = 2
HI = lax.Precision.HIGHEST
F32 = jnp.float32
BF16 = jnp.bfloat16


def place_kernel(routes, slots, children, outgoing, tags, count, sem):
    n = children.shape[0]
    rows = tags.shape[0]

    def clear_tag(i, _):
        tags[i] = 0
        return 0

    lax.fori_loop(0, rows, clear_tag, 0)

    def clear_count(i, _):
        count[i] = 0
        return 0

    lax.fori_loop(0, count.shape[0], clear_count, 0)

    def send(k, _):
        g = routes[k]
        c = count[g]
        count[g] = c + 1
        at = g * CAP + c
        tags[at] = slots[k] + 1
        pltpu.make_async_copy(children.at[k], outgoing.at[at], sem).start()
        return 0

    lax.fori_loop(0, n, send, 0)
    pltpu.make_async_copy(children, outgoing.at[pl.ds(0, n)], sem).wait()


def place(routes, slots, children, groups):
    rows = groups * CAP
    smem = pl.BlockSpec(memory_space=pltpu.SMEM)
    return pl.pallas_call(
        place_kernel,
        out_shape=(
            jax.ShapeDtypeStruct((rows,) + children.shape[1:], children.dtype),
            jax.ShapeDtypeStruct((rows,), jnp.int32),
        ),
        in_specs=[smem, smem, pl.BlockSpec(memory_space=pltpu.VMEM)],
        out_specs=(pl.BlockSpec(memory_space=pl.ANY), smem),
        scratch_shapes=[pltpu.SMEM((groups,), jnp.int32), pltpu.SemaphoreType.DMA],
        name="place",
    )(routes, slots, children)


def assemble_kernel(tags, incoming, base, out, acc):
    side = TILE // SB
    step = pl.program_id(0)
    blocks = incoming.shape[0]

    @pl.when(step == 0)
    def _():
        acc[...] = jnp.zeros_like(acc)

    def add(s, _):
        t = tags[step * blocks + s]

        @pl.when(t > 0)
        def _():
            acc[t - 1] = acc[t - 1] + incoming[s].astype(F32)

        return 0

    lax.fori_loop(0, blocks, add, 0)

    @pl.when(step == pl.num_programs(0) - 1)
    def _():
        for i in range(side):
            for j in range(side):
                rows, cols = slice(i * SB, (i + 1) * SB), slice(j * SB, (j + 1) * SB)
                out[rows, cols] = base[0, rows, cols].astype(F32) + acc[i * side + j]


def assemble(tags, incoming, window):
    steps = 8
    blocks = incoming.shape[0] // steps
    return pl.pallas_call(
        assemble_kernel,
        out_shape=jax.ShapeDtypeStruct((TILE, TILE), F32),
        grid=(steps,),
        in_specs=[
            pl.BlockSpec(memory_space=pltpu.SMEM),
            pl.BlockSpec((blocks, SB, SB), lambda i: (i, 0, 0)),
            pl.BlockSpec((1, TILE, TILE), lambda i: (0, 1, 0)),
        ],
        out_specs=pl.BlockSpec((TILE, TILE), lambda i: (0, 0)),
        scratch_shapes=[pltpu.VMEM(((TILE // SB) ** 2, SB, SB), F32)],
        compiler_params=pltpu.CompilerParams(vmem_limit_bytes=24 << 20),
        name="assemble",
    )(tags, incoming, window)


STEP = 4


def invert_block(block):
    n = block.shape[0]
    s = block
    row_at = lax.broadcasted_iota(jnp.int32, (n, n), 0)
    col_at = lax.broadcasted_iota(jnp.int32, (n, n), 1)
    w = jnp.where(row_at == col_at, 1.0, 0.0).astype(F32)
    done = []
    top = 0
    for j in range(0, n, STEP):
        local = j - top
        cols = [jnp.broadcast_to(s[:, j + a : j + a + 1], s.shape) for a in range(STEP)]
        r = [s[local + a : local + a + 1, :] for a in range(STEP)]
        v = [w[local + a : local + a + 1, :] for a in range(STEP)]
        p = [[cols[b][local + a : local + a + 1, :] for b in range(STEP)] for a in range(STEP)]
        inv = []
        m = [[None] * STEP for _ in range(STEP)]
        for b in range(STEP):
            inv.append(1.0 / p[b][b])
            for a in range(b + 1, STEP):
                m[a][b] = p[a][b] * inv[b]
                for c in range(b + 1, a + 1):
                    p[a][c] = p[a][c] - m[a][b] * p[c][b]
                r[a] = r[a] - m[a][b] * r[b]
                v[a] = v[a] - m[a][b] * v[b]
        done += [v[a] * lax.rsqrt(p[a][a]) for a in range(STEP)]
        if j + STEP >= n:
            break
        y = [None] * STEP
        z = [None] * STEP
        for a in reversed(range(STEP)):
            y[a] = r[a] * inv[a]
            z[a] = v[a] * inv[a]
            for b in range(a + 1, STEP):
                y[a] = y[a] - m[b][a] * y[b]
                z[a] = z[a] - m[b][a] * z[b]
        skip = (j + STEP) // 8 * 8 - top
        s, w = s[skip:], w[skip:]
        cols = [c[skip:] for c in cols]
        top += skip
        if top < j + STEP:
            keep = lax.broadcasted_iota(jnp.int32, s.shape, 0) >= j + STEP - top
            cols = [jnp.where(keep, c, 0.0) for c in cols]
        for a in range(STEP):
            s = s - cols[a] * y[a]
            w = w - cols[a] * z[a]
    return jnp.concatenate(done, axis=0)


def dot(a, b, dims):
    return lax.dot_general(a, b, (dims, ((), ())), precision=HI, preferred_element_type=F32)


def inverse_kernel(pivot, out, work, rest):
    n = pivot.shape[0]
    blocks = n // SB
    row_at = lax.broadcasted_iota(jnp.int32, (n, n), 0)
    col_at = lax.broadcasted_iota(jnp.int32, (n, n), 1)
    work[...] = pivot[...].astype(F32)
    rest[...] = jnp.where(row_at == col_at, 1.0, 0.0).astype(F32)

    def step(k, _):
        here = pl.ds(pl.multiple_of(k * SB, SB), SB)
        block = work[here, here]
        at = [lax.broadcasted_iota(jnp.int32, block.shape, d) for d in (0, 1)]
        small = invert_block(jnp.where(at[0] >= at[1], block, block.T))
        panel = dot(work[:, here], small, ((1,), (1,)))
        below = lax.broadcasted_iota(jnp.int32, (n, SB), 0) >= (k + 1) * SB
        panel = jnp.where(below, panel, 0.0)
        work[...] = work[...] - dot(panel, panel, ((1,), (1,)))
        solved = dot(small, rest[here, :], ((1,), (0,)))
        out[here, :] = solved
        rest[...] = rest[...] - dot(panel, solved, ((1,), (0,)))
        return 0

    lax.fori_loop(0, blocks, step, 0)


def inverse_factor(pivot):
    n = pivot.shape[0]
    vmem = pl.BlockSpec(memory_space=pltpu.VMEM)
    return pl.pallas_call(
        inverse_kernel,
        out_shape=jax.ShapeDtypeStruct((n, n), F32),
        in_specs=[vmem],
        out_specs=vmem,
        scratch_shapes=[pltpu.VMEM((n, n), F32), pltpu.VMEM((n, n), F32)],
        compiler_params=pltpu.CompilerParams(vmem_limit_bytes=24 << 20),
        cost_estimate=pl.CostEstimate(flops=4 * n**3, bytes_accessed=6 * n * n, transcendentals=0),
        name="inverse",
    )(pivot)


def swap(block, axis):
    return lax.all_to_all(block, axis, split_axis=0, concat_axis=0, tiled=True)


HOLDERS = 4


def hand_out(parts, axis, devices):
    mine = jnp.zeros_like(parts[0])
    for part, device in zip(parts, devices):
        if device == 0:
            mine = mine + jnp.where(lax.axis_index(axis) == 0, part, jnp.zeros_like(part))
        else:
            mine = mine + lax.ppermute(part, axis, [(0, device)])
    return mine


def column_holders():
    size = lax.axis_size("col")
    return list(range(0, size, size // HOLDERS))


def to_holders(block):
    parts = list(block.reshape(HOLDERS, -1, block.shape[1]))
    return hand_out(parts, "col", column_holders())


def from_holders(mine):
    size = lax.axis_size("col")
    got = [mine]
    for t in range(1, size):
        got.append(lax.ppermute(mine, "col", [(i, (i - t) % size) for i in column_holders()]))
    return got


def finish_kernel(size, state, *refs):
    halves = refs[:size], refs[size : 2 * size]
    partner, base, added, out = refs[2 * size :]
    column = state[0]
    step = size // HOLDERS
    rows = TILE // HOLDERS
    shift = lax.rem(step - lax.rem(column, step), step)
    first = lax.div(column + shift, step)
    for s in range(step):
        for k in range(HOLDERS):
            source = lax.rem(first + k, HOLDERS)
            at = pl.ds(pl.multiple_of(source * rows, rows), rows)
            under = pl.ds(pl.multiple_of(source * rows + TILE, rows), rows)
            upper_part, under_part = halves[0][k * step + s], halves[1][k * step + s]

            @pl.when((shift == s) & (column == 0))
            def _():
                out[0, at, :] = upper_part[...]
                out[0, under, :] = under_part[...]

            @pl.when((shift == s) & (column != 0))
            def _():
                def product(part):
                    return lax.dot_general(
                        part[...],
                        partner[...],
                        (((1,), (1,)), ((), ())),
                        preferred_element_type=F32,
                    )

                upper = base[0, at, :].astype(F32) - state[1].astype(F32) * product(upper_part)
                out[0, at, :] = upper.astype(BF16)
                lower = added[at, :] - state[2].astype(F32) * product(under_part)
                out[0, under, :] = lower.astype(BF16)


def finish(state, upper, under, partner, window, added):
    size = len(upper)
    vmem = pl.BlockSpec(memory_space=pltpu.VMEM)
    return pl.pallas_call(
        functools.partial(finish_kernel, size),
        out_shape=jax.ShapeDtypeStruct((1, 2 * TILE, TILE), BF16),
        grid=(1,),
        in_specs=[pl.BlockSpec(memory_space=pltpu.SMEM)]
        + [vmem] * (2 * size + 1)
        + [pl.BlockSpec((1, TILE, TILE), lambda i: (0, 0, 0)), vmem],
        out_specs=vmem,
        compiler_params=pltpu.CompilerParams(vmem_limit_bytes=24 << 20),
        name="finish",
    )(state, *upper, *under, partner, window, added)


def shards(window, children, routes, slots, pattern):
    fronts = lax.axis_size("front")
    rows_axis = lax.axis_size("row")
    columns = lax.axis_size("col")
    front = lax.axis_index("front")
    column = lax.axis_index("col")
    first = window[0, :TILE]
    part_rows = TILE // rows_axis
    marks_each = fronts * CAP
    even_raw = swap(first.reshape(rows_axis, part_rows, TILE), "row")[: columns // 2]
    outgoing, marks = place(routes[:, 0], slots, children, fronts * rows_axis)
    marks = marks.reshape(fronts, rows_axis, CAP)
    near = jnp.where(front == 0, marks[0], marks[1])
    far = jnp.where(front == 0, marks[1], marks[0])
    far = lax.ppermute(far, "front", [(0, 1), (1, 0)])
    both = jnp.concatenate([near, far], axis=1).astype(BF16)
    both = jnp.pad(both, ((0, 0), (TILE - marks_each, 0)))[:, None, :]
    place_row = lax.broadcasted_iota(jnp.int32, (rows_axis, part_rows, TILE), 1)
    place_col = lax.broadcasted_iota(jnp.int32, (rows_axis, part_rows, TILE), 2)
    spread = jnp.where(
        (place_row == 0) & (place_col >= TILE - marks_each), both, even_raw[0][None]
    )
    pivot = swap(spread, "row")
    got = pivot[:, 0, TILE - marks_each :].astype(jnp.int32).reshape(rows_axis, fronts, CAP)
    near, far = got[:, 0], got[:, 1]
    tags = jnp.stack([jnp.where(front == 0, near, far), jnp.where(front == 0, far, near)])
    tags = tags.reshape(-1)
    pivot = pivot.reshape(TILE, TILE)
    outgoing, tags, pivot = lax.optimization_barrier((outgoing, tags, pivot))
    incoming = swap(outgoing, ("front", "row"))
    inverse = inverse_factor(pivot)

    def solve(rows):
        return lax.dot_general(
            rows.astype(F32), inverse, (((1,), (1,)), ((), ())), precision=HI
        ).astype(BF16)

    even = solve(even_raw.reshape(-1, TILE)).reshape(even_raw.shape)
    even_part = hand_out(list(even), "col", range(0, columns, 2))
    upper = from_holders(to_holders(solve(first)))
    incoming, even_part, upper = lax.optimization_barrier((incoming, even_part, upper))
    added = assemble(tags, incoming, window)
    lower_second = solve(added)
    odd = swap(lower_second.reshape(rows_axis, part_rows, TILE), "row")
    under = to_holders(lower_second)
    odd, under = lax.optimization_barrier((odd, under))
    odd_part = hand_out(list(odd[: columns // 2]), "col", range(1, columns, 2))
    under = from_holders(under)
    partner_part = jnp.where(column % 2 == 0, even_part, odd_part)
    partner = swap(
        jnp.broadcast_to(partner_part[None], (rows_axis,) + partner_part.shape), "row"
    ).reshape(TILE, TILE)

    state = jnp.concatenate([jnp.full((1,), column, jnp.int32), pattern[0, :, 0]])
    return finish(state, upper, under, partner, window, added)


def solution(mesh):
    placed = (
        P("front", "row", "col"),
        P(("front", "row", "col"), None, None),
        P(("front", "row", "col"), None),
        P(("front", "row", "col")),
        P("front", "row", "col"),
    )
    return jax.shard_map(
        shards, mesh=mesh, in_specs=placed, out_specs=P("front", "row", "col"), check_vma=False
    )
```

```python
import functools

import jax
import jax.numpy as jnp
from jax import lax
from jax.experimental import pallas as pl
from jax.experimental.pallas import tpu as pltpu
from jax.sharding import PartitionSpec as P

TILE = 512
SB = 128
CAP = 2
HI = lax.Precision.HIGHEST
F32 = jnp.float32
BF16 = jnp.bfloat16


def place_kernel(routes, slots, children, outgoing, tags, count, sem):
    n = children.shape[0]
    rows = tags.shape[0]

    def clear_tag(i, _):
        tags[i] = 0
        return 0

    lax.fori_loop(0, rows, clear_tag, 0)

    def clear_count(i, _):
        count[i] = 0
        return 0

    lax.fori_loop(0, count.shape[0], clear_count, 0)

    def send(k, _):
        g = routes[k]
        c = count[g]
        count[g] = c + 1
        at = g * CAP + c
        tags[at] = slots[k] + 1
        pltpu.make_async_copy(children.at[k], outgoing.at[at], sem).start()
        return 0

    lax.fori_loop(0, n, send, 0)
    pltpu.make_async_copy(children, outgoing.at[pl.ds(0, n)], sem).wait()


def place(routes, slots, children, groups):
    rows = groups * CAP
    smem = pl.BlockSpec(memory_space=pltpu.SMEM)
    return pl.pallas_call(
        place_kernel,
        out_shape=(
            jax.ShapeDtypeStruct((rows,) + children.shape[1:], children.dtype),
            jax.ShapeDtypeStruct((rows,), jnp.int32),
        ),
        in_specs=[smem, smem, pl.BlockSpec(memory_space=pltpu.VMEM)],
        out_specs=(pl.BlockSpec(memory_space=pl.ANY), smem),
        scratch_shapes=[pltpu.SMEM((groups,), jnp.int32), pltpu.SemaphoreType.DMA],
        name="place",
    )(routes, slots, children)


def assemble_kernel(tags, incoming, base, out, acc):
    side = TILE // SB
    step = pl.program_id(0)
    blocks = incoming.shape[0]

    @pl.when(step == 0)
    def _():
        acc[...] = jnp.zeros_like(acc)

    def add(s, _):
        t = tags[step * blocks + s]

        @pl.when(t > 0)
        def _():
            acc[t - 1] = acc[t - 1] + incoming[s].astype(F32)

        return 0

    lax.fori_loop(0, blocks, add, 0)

    @pl.when(step == pl.num_programs(0) - 1)
    def _():
        for i in range(side):
            for j in range(side):
                rows, cols = slice(i * SB, (i + 1) * SB), slice(j * SB, (j + 1) * SB)
                out[rows, cols] = base[0, rows, cols].astype(F32) + acc[i * side + j]


def assemble(tags, incoming, window):
    steps = 1
    blocks = incoming.shape[0] // steps
    return pl.pallas_call(
        assemble_kernel,
        out_shape=jax.ShapeDtypeStruct((TILE, TILE), F32),
        grid=(steps,),
        in_specs=[
            pl.BlockSpec(memory_space=pltpu.SMEM),
            pl.BlockSpec((blocks, SB, SB), lambda i: (i, 0, 0)),
            pl.BlockSpec((1, TILE, TILE), lambda i: (0, 1, 0)),
        ],
        out_specs=pl.BlockSpec((TILE, TILE), lambda i: (0, 0)),
        scratch_shapes=[pltpu.VMEM(((TILE // SB) ** 2, SB, SB), F32)],
        compiler_params=pltpu.CompilerParams(vmem_limit_bytes=24 << 20),
        name="assemble",
    )(tags, incoming, window)


STEP = 4


def invert_block(block):
    n = block.shape[0]
    s = block
    row_at = lax.broadcasted_iota(jnp.int32, (n, n), 0)
    col_at = lax.broadcasted_iota(jnp.int32, (n, n), 1)
    w = jnp.where(row_at == col_at, 1.0, 0.0).astype(F32)
    done = []
    top = 0
    for j in range(0, n, STEP):
        local = j - top
        cols = [jnp.broadcast_to(s[:, j + a : j + a + 1], s.shape) for a in range(STEP)]
        r = [s[local + a : local + a + 1, :] for a in range(STEP)]
        v = [w[local + a : local + a + 1, :] for a in range(STEP)]
        p = [[cols[b][local + a : local + a + 1, :] for b in range(STEP)] for a in range(STEP)]
        inv = []
        m = [[None] * STEP for _ in range(STEP)]
        for b in range(STEP):
            inv.append(1.0 / p[b][b])
            for a in range(b + 1, STEP):
                m[a][b] = p[a][b] * inv[b]
                for c in range(b + 1, a + 1):
                    p[a][c] = p[a][c] - m[a][b] * p[c][b]
                r[a] = r[a] - m[a][b] * r[b]
                v[a] = v[a] - m[a][b] * v[b]
        done += [v[a] * lax.rsqrt(p[a][a]) for a in range(STEP)]
        if j + STEP >= n:
            break
        y = [None] * STEP
        z = [None] * STEP
        for a in reversed(range(STEP)):
            y[a] = r[a] * inv[a]
            z[a] = v[a] * inv[a]
            for b in range(a + 1, STEP):
                y[a] = y[a] - m[b][a] * y[b]
                z[a] = z[a] - m[b][a] * z[b]
        skip = (j + STEP) // 8 * 8 - top
        s, w = s[skip:], w[skip:]
        cols = [c[skip:] for c in cols]
        top += skip
        if top < j + STEP:
            keep = lax.broadcasted_iota(jnp.int32, s.shape, 0) >= j + STEP - top
            cols = [jnp.where(keep, c, 0.0) for c in cols]
        for a in range(STEP):
            s = s - cols[a] * y[a]
            w = w - cols[a] * z[a]
    return jnp.concatenate(done, axis=0)


def dot(a, b, dims):
    return lax.dot_general(a, b, (dims, ((), ())), precision=HI, preferred_element_type=F32)


def lower_blocks(n):
    return [(i, j) for i in range(n // SB) for j in range(i + 1)]


def inverse_kernel(packed, out, work, rest):
    n = out.shape[0]
    row_at = lax.broadcasted_iota(jnp.int32, (n, n), 0)
    col_at = lax.broadcasted_iota(jnp.int32, (n, n), 1)
    work[...] = jnp.zeros_like(work)
    for at, (i, j) in enumerate(lower_blocks(n)):
        work[i * SB : (i + 1) * SB, j * SB : (j + 1) * SB] = packed[
            at * SB : (at + 1) * SB, :
        ].astype(F32)
    rest[...] = jnp.where(row_at == col_at, 1.0, 0.0).astype(F32)

    def step(k, _):
        here = pl.ds(pl.multiple_of(k * SB, SB), SB)
        small = invert_block(work[here, here])
        panel = dot(work[:, here], small, ((1,), (1,)))
        below = lax.broadcasted_iota(jnp.int32, (n, SB), 0) >= (k + 1) * SB
        panel = jnp.where(below, panel, 0.0)
        work[...] = work[...] - dot(panel, panel, ((1,), (1,)))
        solved = dot(small, rest[here, :], ((1,), (0,)))
        out[here, :] = solved
        rest[...] = rest[...] - dot(panel, solved, ((1,), (0,)))
        return 0

    lax.fori_loop(0, n // SB, step, 0)


def inverse_factor(packed):
    n = TILE
    vmem = pl.BlockSpec(memory_space=pltpu.VMEM)
    return pl.pallas_call(
        inverse_kernel,
        out_shape=jax.ShapeDtypeStruct((n, n), F32),
        in_specs=[vmem],
        out_specs=vmem,
        scratch_shapes=[pltpu.VMEM((n, n), F32), pltpu.VMEM((n, n), F32)],
        compiler_params=pltpu.CompilerParams(vmem_limit_bytes=24 << 20),
        cost_estimate=pl.CostEstimate(flops=4 * n**3, bytes_accessed=6 * n * n, transcendentals=0),
        name="inverse",
    )(packed)


def pack_kernel(base, out):
    for at, (i, j) in enumerate(lower_blocks(TILE)):
        out[at * SB : (at + 1) * SB, :] = base[0, i * SB : (i + 1) * SB, j * SB : (j + 1) * SB]


def pack_pivot(window):
    rows = len(lower_blocks(TILE)) * SB
    return pl.pallas_call(
        pack_kernel,
        out_shape=jax.ShapeDtypeStruct((rows, SB), window.dtype),
        grid=(1,),
        in_specs=[pl.BlockSpec((1, TILE, TILE), lambda i: (0, 0, 0))],
        out_specs=pl.BlockSpec((rows, SB), lambda i: (0, 0)),
        name="pack",
    )(window)


def swap(block, axis):
    return lax.all_to_all(block, axis, split_axis=0, concat_axis=0, tiled=True)


HOLDERS = 4


def hand_out(parts, axis, devices):
    mine = jnp.zeros_like(parts[0])
    for part, device in zip(parts, devices):
        if device == 0:
            mine = mine + jnp.where(lax.axis_index(axis) == 0, part, jnp.zeros_like(part))
        else:
            mine = mine + lax.ppermute(part, axis, [(0, device)])
    return mine


def column_holders():
    size = lax.axis_size("col")
    return list(range(0, size, size // HOLDERS))


def to_holders(block):
    parts = list(block.reshape(HOLDERS, -1, block.shape[1]))
    return hand_out(parts, "col", column_holders())


def from_holders(mine):
    size = lax.axis_size("col")
    got = [mine]
    for t in range(1, size):
        got.append(lax.ppermute(mine, "col", [(i, (i - t) % size) for i in column_holders()]))
    return got


def finish_kernel(size, state, *refs):
    halves = refs[:size], refs[size : 2 * size]
    partner, base, added, out, parts, sem = refs[2 * size :]
    column = state[0]
    step = size // HOLDERS
    rows = TILE // HOLDERS
    shift = lax.rem(step - lax.rem(column, step), step)
    first = lax.div(column + shift, step)
    for s in range(step):

        @pl.when(shift == s)
        def _():
            copies = [
                pltpu.make_async_copy(
                    halves[h][k * step + s], parts.at[h, k], sem.at[h * HOLDERS + k]
                )
                for h in range(2)
                for k in range(HOLDERS)
            ]
            for copy in copies:
                copy.start()
            for copy in copies:
                copy.wait()

    for k in range(HOLDERS):
        source = lax.rem(first + k, HOLDERS)
        at = pl.ds(pl.multiple_of(source * rows, rows), rows)
        under = pl.ds(pl.multiple_of(source * rows + TILE, rows), rows)

        @pl.when(column == 0)
        def _():
            out[0, at, :] = parts[0, k]
            out[0, under, :] = parts[1, k]

        @pl.when(column != 0)
        def _():
            def product(part):
                return lax.dot_general(
                    part, partner[...], (((1,), (1,)), ((), ())), preferred_element_type=F32
                )

            upper = base[0, at, :].astype(F32) - state[1].astype(F32) * product(parts[0, k])
            out[0, at, :] = upper.astype(BF16)
            lower = added[at, :] - state[2].astype(F32) * product(parts[1, k])
            out[0, under, :] = lower.astype(BF16)


def finish(state, upper, under, partner, window, added):
    size = len(upper)

    def whole(x):
        return pl.BlockSpec(x.shape, lambda i: (0,) * x.ndim)

    tile = pl.BlockSpec((1, TILE, TILE), lambda i: (0, 0, 0))
    out = jax.ShapeDtypeStruct((1, 2 * TILE, TILE), BF16)
    return pl.pallas_call(
        functools.partial(finish_kernel, size),
        out_shape=out,
        grid=(1,),
        in_specs=[pl.BlockSpec(memory_space=pltpu.SMEM)]
        + [pl.BlockSpec(memory_space=pl.ANY)] * (2 * size)
        + [whole(partner), tile, whole(added)],
        out_specs=whole(out),
        scratch_shapes=[
            pltpu.VMEM((2, HOLDERS, TILE // HOLDERS, TILE), BF16),
            pltpu.SemaphoreType.DMA((2 * HOLDERS,)),
        ],
        compiler_params=pltpu.CompilerParams(vmem_limit_bytes=56 << 20),
        name="finish",
    )(state, *upper, *under, partner, window, added)


def shards(window, children, routes, slots, pattern):
    fronts = lax.axis_size("front")
    rows_axis = lax.axis_size("row")
    columns = lax.axis_size("col")
    front = lax.axis_index("front")
    column = lax.axis_index("col")
    first = window[0, :TILE]
    packed = pack_pivot(window).reshape(rows_axis, -1, SB)
    share = packed.shape[1]
    pivot_part = swap(packed, "row")[0]
    outgoing, marks = place(routes[:, 0], slots, children, fronts * rows_axis)
    marks = marks.reshape(fronts, rows_axis, CAP)
    near = jnp.where(front == 0, marks[0], marks[1])
    far = jnp.where(front == 0, marks[1], marks[0])
    far = lax.ppermute(far, "front", [(0, 1), (1, 0)])
    both = jnp.concatenate([near, far], axis=1).astype(BF16)[:, None, :]
    both = jnp.pad(both, ((0, 0), (share, 7), (0, SB - both.shape[2])))
    piece = jnp.pad(pivot_part, ((0, 8), (0, 0)))[None]
    row_at = lax.broadcasted_iota(jnp.int32, both.shape, 1)
    arrived = swap(jnp.where(row_at < share, piece, both), "row")
    got = arrived[:, share, : fronts * CAP].astype(jnp.int32).reshape(rows_axis, fronts, CAP)
    near, far = got[:, 0], got[:, 1]
    tags = jnp.stack([jnp.where(front == 0, near, far), jnp.where(front == 0, far, near)])
    tags = tags.reshape(-1)
    pivot = arrived[:, :share].reshape(-1, SB)
    outgoing, tags, pivot = lax.optimization_barrier((outgoing, tags, pivot))
    incoming = swap(outgoing, ("front", "row"))
    inverse = inverse_factor(pivot)

    def solve(rows):
        return lax.dot_general(
            rows.astype(F32), inverse, (((1,), (1,)), ((), ())), precision=HI
        ).astype(BF16)

    def to_plane(lower, odd):
        pairs = [
            ((c // 2) * columns, (c // 2) * columns + c) for c in range(max(odd, 1), columns) if c % 2 == odd
        ]
        return lax.ppermute(lower, ("row", "col"), pairs)

    lower_first = solve(first)
    even = to_plane(lower_first, 0)
    upper = from_holders(to_holders(lower_first))
    incoming, even, upper = lax.optimization_barrier((incoming, even, upper))
    added = assemble(tags, incoming, window)
    lower_second = solve(added)
    odd = to_plane(lower_second, 1)
    piece = jnp.where(column % 2 == 0, even, odd)
    piece, under = lax.optimization_barrier((piece, to_holders(lower_second)))
    under = from_holders(under)
    got = swap(piece.reshape(rows_axis, -1, TILE), "row")
    got, *under[: HOLDERS + 1] = lax.optimization_barrier((got, *under[: HOLDERS + 1]))
    owned = lax.dynamic_index_in_dim(got, column // 2, 0)
    partner = swap(jnp.broadcast_to(owned, got.shape), "row").reshape(TILE, TILE)
    state = jnp.concatenate([jnp.full((1,), column, jnp.int32), pattern[0, :, 0]])
    return finish(state, upper, under, partner, window, added)


def solution(mesh):
    placed = (
        P("front", "row", "col"),
        P(("front", "row", "col"), None, None),
        P(("front", "row", "col"), None),
        P(("front", "row", "col")),
        P("front", "row", "col"),
    )
    return jax.shard_map(
        shards, mesh=mesh, in_specs=placed, out_specs=P("front", "row", "col"), check_vma=False
    )
```

```python
import functools

import jax
import jax.numpy as jnp
from jax import lax
from jax.experimental import pallas as pl
from jax.experimental.pallas import tpu as pltpu
from jax.sharding import PartitionSpec as P

TILE = 512
SB = 128
CAP = 2
HI = lax.Precision.HIGHEST
F32 = jnp.float32
BF16 = jnp.bfloat16


def place_kernel(routes, slots, children, outgoing, tags, count, sem):
    n = children.shape[0]
    rows = tags.shape[0]

    def clear_tag(i, _):
        tags[i] = 0
        return 0

    lax.fori_loop(0, rows, clear_tag, 0)

    def clear_count(i, _):
        count[i] = 0
        return 0

    lax.fori_loop(0, count.shape[0], clear_count, 0)

    def send(k, _):
        g = routes[k]
        c = count[g]
        count[g] = c + 1
        at = g * CAP + c
        tags[at] = slots[k] + 1
        pltpu.make_async_copy(children.at[k], outgoing.at[at], sem).start()
        return 0

    lax.fori_loop(0, n, send, 0)
    pltpu.make_async_copy(children, outgoing.at[pl.ds(0, n)], sem).wait()


def place(routes, slots, children, groups):
    rows = groups * CAP
    smem = pl.BlockSpec(memory_space=pltpu.SMEM)
    return pl.pallas_call(
        place_kernel,
        out_shape=(
            jax.ShapeDtypeStruct((rows,) + children.shape[1:], children.dtype),
            jax.ShapeDtypeStruct((rows,), jnp.int32),
        ),
        in_specs=[smem, smem, pl.BlockSpec(memory_space=pltpu.VMEM)],
        out_specs=(pl.BlockSpec(memory_space=pl.ANY), smem),
        scratch_shapes=[pltpu.SMEM((groups,), jnp.int32), pltpu.SemaphoreType.DMA],
        name="place",
    )(routes, slots, children)


def assemble_kernel(tags, incoming, base, out, acc):
    side = TILE // SB
    step = pl.program_id(0)
    blocks = incoming.shape[0]

    @pl.when(step == 0)
    def _():
        acc[...] = jnp.zeros_like(acc)

    def add(s, _):
        t = tags[step * blocks + s]

        @pl.when(t > 0)
        def _():
            acc[t - 1] = acc[t - 1] + incoming[s].astype(F32)

        return 0

    lax.fori_loop(0, blocks, add, 0)

    @pl.when(step == pl.num_programs(0) - 1)
    def _():
        for i in range(side):
            for j in range(side):
                rows, cols = slice(i * SB, (i + 1) * SB), slice(j * SB, (j + 1) * SB)
                out[rows, cols] = base[0, rows, cols].astype(F32) + acc[i * side + j]


def assemble(tags, incoming, window):
    steps = 1
    blocks = incoming.shape[0] // steps
    return pl.pallas_call(
        assemble_kernel,
        out_shape=jax.ShapeDtypeStruct((TILE, TILE), F32),
        grid=(steps,),
        in_specs=[
            pl.BlockSpec(memory_space=pltpu.SMEM),
            pl.BlockSpec((blocks, SB, SB), lambda i: (i, 0, 0)),
            pl.BlockSpec((1, TILE, TILE), lambda i: (0, 1, 0)),
        ],
        out_specs=pl.BlockSpec((TILE, TILE), lambda i: (0, 0)),
        scratch_shapes=[pltpu.VMEM(((TILE // SB) ** 2, SB, SB), F32)],
        compiler_params=pltpu.CompilerParams(vmem_limit_bytes=24 << 20),
        name="assemble",
    )(tags, incoming, window)


STEP = 4


def invert_block(block):
    n = block.shape[0]
    s = block
    row_at = lax.broadcasted_iota(jnp.int32, (n, n), 0)
    col_at = lax.broadcasted_iota(jnp.int32, (n, n), 1)
    w = jnp.where(row_at == col_at, 1.0, 0.0).astype(F32)
    done = []
    top = 0
    for j in range(0, n, STEP):
        local = j - top
        cols = [jnp.broadcast_to(s[:, j + a : j + a + 1], s.shape) for a in range(STEP)]
        r = [s[local + a : local + a + 1, :] for a in range(STEP)]
        v = [w[local + a : local + a + 1, :] for a in range(STEP)]
        p = [[cols[b][local + a : local + a + 1, :] for b in range(STEP)] for a in range(STEP)]
        inv = []
        m = [[None] * STEP for _ in range(STEP)]
        for b in range(STEP):
            inv.append(1.0 / p[b][b])
            for a in range(b + 1, STEP):
                m[a][b] = p[a][b] * inv[b]
                for c in range(b + 1, a + 1):
                    p[a][c] = p[a][c] - m[a][b] * p[c][b]
                r[a] = r[a] - m[a][b] * r[b]
                v[a] = v[a] - m[a][b] * v[b]
        done += [v[a] * lax.rsqrt(p[a][a]) for a in range(STEP)]
        if j + STEP >= n:
            break
        y = [None] * STEP
        z = [None] * STEP
        for a in reversed(range(STEP)):
            y[a] = r[a] * inv[a]
            z[a] = v[a] * inv[a]
            for b in range(a + 1, STEP):
                y[a] = y[a] - m[b][a] * y[b]
                z[a] = z[a] - m[b][a] * z[b]
        skip = (j + STEP) // 8 * 8 - top
        s, w = s[skip:], w[skip:]
        cols = [c[skip:] for c in cols]
        top += skip
        if top < j + STEP:
            keep = lax.broadcasted_iota(jnp.int32, s.shape, 0) >= j + STEP - top
            cols = [jnp.where(keep, c, 0.0) for c in cols]
        for a in range(STEP):
            s = s - cols[a] * y[a]
            w = w - cols[a] * z[a]
    return jnp.concatenate(done, axis=0)


def dot(a, b, dims):
    return lax.dot_general(a, b, (dims, ((), ())), precision=HI, preferred_element_type=F32)


def lower_blocks(n):
    return [(i, j) for i in range(n // SB) for j in range(i + 1)]


def inverse_kernel(packed, out, work, rest):
    n = out.shape[0]
    row_at = lax.broadcasted_iota(jnp.int32, (n, n), 0)
    col_at = lax.broadcasted_iota(jnp.int32, (n, n), 1)
    work[...] = jnp.zeros_like(work)
    for at, (i, j) in enumerate(lower_blocks(n)):
        work[i * SB : (i + 1) * SB, j * SB : (j + 1) * SB] = packed[
            at * SB : (at + 1) * SB, :
        ].astype(F32)
    rest[...] = jnp.where(row_at == col_at, 1.0, 0.0).astype(F32)

    def step(k, _):
        here = pl.ds(pl.multiple_of(k * SB, SB), SB)
        small = invert_block(work[here, here])
        panel = dot(work[:, here], small, ((1,), (1,)))
        below = lax.broadcasted_iota(jnp.int32, (n, SB), 0) >= (k + 1) * SB
        panel = jnp.where(below, panel, 0.0)
        work[...] = work[...] - dot(panel, panel, ((1,), (1,)))
        solved = dot(small, rest[here, :], ((1,), (0,)))
        out[here, :] = solved
        rest[...] = rest[...] - dot(panel, solved, ((1,), (0,)))
        return 0

    lax.fori_loop(0, n // SB, step, 0)


def inverse_factor(packed):
    n = TILE
    vmem = pl.BlockSpec(memory_space=pltpu.VMEM)
    return pl.pallas_call(
        inverse_kernel,
        out_shape=jax.ShapeDtypeStruct((n, n), F32),
        in_specs=[vmem],
        out_specs=vmem,
        scratch_shapes=[pltpu.VMEM((n, n), F32), pltpu.VMEM((n, n), F32)],
        compiler_params=pltpu.CompilerParams(vmem_limit_bytes=24 << 20),
        cost_estimate=pl.CostEstimate(flops=4 * n**3, bytes_accessed=6 * n * n, transcendentals=0),
        name="inverse",
    )(packed)


def pack_kernel(base, out):
    for at, (i, j) in enumerate(lower_blocks(TILE)):
        out[at * SB : (at + 1) * SB, :] = base[0, i * SB : (i + 1) * SB, j * SB : (j + 1) * SB]


def pack_pivot(window):
    rows = len(lower_blocks(TILE)) * SB
    return pl.pallas_call(
        pack_kernel,
        out_shape=jax.ShapeDtypeStruct((rows, SB), window.dtype),
        grid=(1,),
        in_specs=[pl.BlockSpec((1, TILE, TILE), lambda i: (0, 0, 0))],
        out_specs=pl.BlockSpec((rows, SB), lambda i: (0, 0)),
        name="pack",
    )(window)


def swap(block, axis):
    return lax.all_to_all(block, axis, split_axis=0, concat_axis=0, tiled=True)


def to_columns(block):
    size = lax.axis_size("col")
    got = [None] * size
    for step in range(1, size):
        c = (step + 1) // 2 if step % 2 else size - step // 2
        got[c] = lax.ppermute(block, "col", [(0, c)])
    got[0] = block
    return got


def finish_kernel(size, state, *refs):
    halves = refs[:size], refs[size : 2 * size]
    partner, base, added, out, tiles, sem = refs[2 * size :]
    column = state[0]
    for c in range(size):

        @pl.when(column == c)
        def _():
            copies = [
                pltpu.make_async_copy(halves[h][c], tiles.at[h], sem.at[h]) for h in range(2)
            ]
            for copy in copies:
                copy.start()
            for copy in copies:
                copy.wait()

    @pl.when(column == 0)
    def _():
        out[0, :TILE, :] = tiles[0]
        out[0, TILE:, :] = tiles[1]

    @pl.when(column != 0)
    def _():
        def product(tile):
            return lax.dot_general(
                tile, partner[...], (((1,), (1,)), ((), ())), preferred_element_type=F32
            )

        upper = base[0].astype(F32) - state[1].astype(F32) * product(tiles[0])
        out[0, :TILE, :] = upper.astype(BF16)
        lower = added[...] - state[2].astype(F32) * product(tiles[1])
        out[0, TILE:, :] = lower.astype(BF16)


def finish(state, upper, under, partner, window, added):
    size = len(upper)

    def whole(x):
        return pl.BlockSpec(x.shape, lambda i: (0,) * x.ndim)

    tile = pl.BlockSpec((1, TILE, TILE), lambda i: (0, 0, 0))
    out = jax.ShapeDtypeStruct((1, 2 * TILE, TILE), BF16)
    return pl.pallas_call(
        functools.partial(finish_kernel, size),
        out_shape=out,
        grid=(1,),
        in_specs=[pl.BlockSpec(memory_space=pltpu.SMEM)]
        + [pl.BlockSpec(memory_space=pl.ANY)] * (2 * size)
        + [whole(partner), tile, whole(added)],
        out_specs=whole(out),
        scratch_shapes=[
            pltpu.VMEM((2, TILE, TILE), BF16),
            pltpu.SemaphoreType.DMA((2,)),
        ],
        compiler_params=pltpu.CompilerParams(vmem_limit_bytes=56 << 20),
        name="finish",
    )(state, *upper, *under, partner, window, added)


def shards(window, children, routes, slots, pattern):
    fronts = lax.axis_size("front")
    rows_axis = lax.axis_size("row")
    columns = lax.axis_size("col")
    front = lax.axis_index("front")
    column = lax.axis_index("col")
    first = window[0, :TILE]
    packed = pack_pivot(window).reshape(rows_axis, -1, SB)
    share = packed.shape[1]
    pivot_part = swap(packed, "row")[0]
    outgoing, marks = place(routes[:, 0], slots, children, fronts * rows_axis)
    marks = marks.reshape(fronts, rows_axis, CAP)
    near = jnp.where(front == 0, marks[0], marks[1])
    far = jnp.where(front == 0, marks[1], marks[0])
    far = lax.ppermute(far, "front", [(0, 1), (1, 0)])
    both = jnp.concatenate([near, far], axis=1).astype(BF16)[:, None, :]
    both = jnp.pad(both, ((0, 0), (share, 7), (0, SB - both.shape[2])))
    piece = jnp.pad(pivot_part, ((0, 8), (0, 0)))[None]
    row_at = lax.broadcasted_iota(jnp.int32, both.shape, 1)
    arrived = swap(jnp.where(row_at < share, piece, both), "row")
    got = arrived[:, share, : fronts * CAP].astype(jnp.int32).reshape(rows_axis, fronts, CAP)
    near, far = got[:, 0], got[:, 1]
    tags = jnp.stack([jnp.where(front == 0, near, far), jnp.where(front == 0, far, near)])
    tags = tags.reshape(-1)
    pivot = arrived[:, :share].reshape(-1, SB)
    outgoing, tags, pivot = lax.optimization_barrier((outgoing, tags, pivot))
    incoming = swap(outgoing, ("front", "row"))
    inverse = inverse_factor(pivot)

    def solve(rows):
        return lax.dot_general(
            rows.astype(F32), inverse, (((1,), (1,)), ((), ())), precision=HI
        ).astype(BF16)

    def to_plane(lower, odd):
        planes = [c for c in range(1, columns) if c % 2 == odd]
        pairs = [((c // 2) * columns, (c // 2) * columns + c) for c in planes]
        return lax.ppermute(lower, ("row", "col"), pairs)

    lower_first = solve(first)
    even = to_plane(lower_first, 0)
    upper = to_columns(lower_first)
    incoming, even, upper = lax.optimization_barrier((incoming, even, upper))
    added = assemble(tags, incoming, window)
    lower_second = solve(added)
    odd = to_plane(lower_second, 1)
    piece = jnp.where(column % 2 == 0, even, odd)
    under = to_columns(lower_second)
    got = swap(piece.reshape(rows_axis, -1, TILE), "row")
    early = [1, columns - 1, 2, columns - 2]
    got, *arrived = lax.optimization_barrier((got, *(under[c] for c in early)))
    for c, tile in zip(early, arrived):
        under[c] = tile
    owned = lax.dynamic_index_in_dim(got, column // 2, 0)
    partner = swap(jnp.broadcast_to(owned, got.shape), "row").reshape(TILE, TILE)
    state = jnp.concatenate([jnp.full((1,), column, jnp.int32), pattern[0, :, 0]])
    return finish(state, upper, under, partner, window, added)


def solution(mesh):
    placed = (
        P("front", "row", "col"),
        P(("front", "row", "col"), None, None),
        P(("front", "row", "col"), None),
        P(("front", "row", "col")),
        P("front", "row", "col"),
    )
    return jax.shard_map(
        shards, mesh=mesh, in_specs=placed, out_specs=P("front", "row", "col"), check_vma=False
    )
```

```python
import functools

import jax
import jax.numpy as jnp
from jax import lax
from jax.experimental import pallas as pl
from jax.experimental.pallas import tpu as pltpu
from jax.sharding import PartitionSpec as P

TILE = 512
SB = 128
CAP = 2
HI = lax.Precision.HIGHEST
F32 = jnp.float32
BF16 = jnp.bfloat16


def place_kernel(routes, slots, children, outgoing, tags, count, sem):
    n = children.shape[0]
    rows = tags.shape[0]

    def clear_tag(i, _):
        tags[i] = 0
        return 0

    lax.fori_loop(0, rows, clear_tag, 0)

    def clear_count(i, _):
        count[i] = 0
        return 0

    lax.fori_loop(0, count.shape[0], clear_count, 0)

    def send(k, _):
        g = routes[k]
        c = count[g]
        count[g] = c + 1
        at = g * CAP + c
        tags[at] = slots[k] + 1
        pltpu.make_async_copy(children.at[k], outgoing.at[at], sem).start()
        return 0

    lax.fori_loop(0, n, send, 0)
    pltpu.make_async_copy(children, outgoing.at[pl.ds(0, n)], sem).wait()


def place(routes, slots, children, groups):
    rows = groups * CAP
    smem = pl.BlockSpec(memory_space=pltpu.SMEM)
    return pl.pallas_call(
        place_kernel,
        out_shape=(
            jax.ShapeDtypeStruct((rows,) + children.shape[1:], children.dtype),
            jax.ShapeDtypeStruct((rows,), jnp.int32),
        ),
        in_specs=[smem, smem, pl.BlockSpec(memory_space=pltpu.VMEM)],
        out_specs=(pl.BlockSpec(memory_space=pl.ANY), smem),
        scratch_shapes=[pltpu.SMEM((groups,), jnp.int32), pltpu.SemaphoreType.DMA],
        name="place",
    )(routes, slots, children)


def assemble_kernel(tags, incoming, base, out, acc):
    side = TILE // SB
    step = pl.program_id(0)
    blocks = incoming.shape[0]

    @pl.when(step == 0)
    def _():
        acc[...] = jnp.zeros_like(acc)

    def add(s, _):
        t = tags[step * blocks + s]

        @pl.when(t > 0)
        def _():
            acc[t - 1] = acc[t - 1] + incoming[s].astype(F32)

        return 0

    lax.fori_loop(0, blocks, add, 0)

    @pl.when(step == pl.num_programs(0) - 1)
    def _():
        for i in range(side):
            for j in range(side):
                rows, cols = slice(i * SB, (i + 1) * SB), slice(j * SB, (j + 1) * SB)
                out[rows, cols] = base[0, rows, cols].astype(F32) + acc[i * side + j]


def assemble(tags, incoming, window):
    steps = 1
    blocks = incoming.shape[0] // steps
    return pl.pallas_call(
        assemble_kernel,
        out_shape=jax.ShapeDtypeStruct((TILE, TILE), F32),
        grid=(steps,),
        in_specs=[
            pl.BlockSpec(memory_space=pltpu.SMEM),
            pl.BlockSpec((blocks, SB, SB), lambda i: (i, 0, 0)),
            pl.BlockSpec((1, TILE, TILE), lambda i: (0, 1, 0)),
        ],
        out_specs=pl.BlockSpec((TILE, TILE), lambda i: (0, 0)),
        scratch_shapes=[pltpu.VMEM(((TILE // SB) ** 2, SB, SB), F32)],
        compiler_params=pltpu.CompilerParams(vmem_limit_bytes=24 << 20),
        name="assemble",
    )(tags, incoming, window)


STEP = 4


def invert_block(block):
    n = block.shape[0]
    s = block
    row_at = lax.broadcasted_iota(jnp.int32, (n, n), 0)
    col_at = lax.broadcasted_iota(jnp.int32, (n, n), 1)
    w = jnp.where(row_at == col_at, 1.0, 0.0).astype(F32)
    done = []
    top = 0
    for j in range(0, n, STEP):
        local = j - top
        cols = [jnp.broadcast_to(s[:, j + a : j + a + 1], s.shape) for a in range(STEP)]
        r = [s[local + a : local + a + 1, :] for a in range(STEP)]
        v = [w[local + a : local + a + 1, :] for a in range(STEP)]
        p = [[cols[b][local + a : local + a + 1, :] for b in range(STEP)] for a in range(STEP)]
        inv = []
        m = [[None] * STEP for _ in range(STEP)]
        for b in range(STEP):
            inv.append(1.0 / p[b][b])
            for a in range(b + 1, STEP):
                m[a][b] = p[a][b] * inv[b]
                for c in range(b + 1, a + 1):
                    p[a][c] = p[a][c] - m[a][b] * p[c][b]
                r[a] = r[a] - m[a][b] * r[b]
                v[a] = v[a] - m[a][b] * v[b]
        done += [v[a] * lax.rsqrt(p[a][a]) for a in range(STEP)]
        if j + STEP >= n:
            break
        y = [None] * STEP
        z = [None] * STEP
        for a in reversed(range(STEP)):
            y[a] = r[a] * inv[a]
            z[a] = v[a] * inv[a]
            for b in range(a + 1, STEP):
                y[a] = y[a] - m[b][a] * y[b]
                z[a] = z[a] - m[b][a] * z[b]
        skip = (j + STEP) // 8 * 8 - top
        s, w = s[skip:], w[skip:]
        cols = [c[skip:] for c in cols]
        top += skip
        if top < j + STEP:
            keep = lax.broadcasted_iota(jnp.int32, s.shape, 0) >= j + STEP - top
            cols = [jnp.where(keep, c, 0.0) for c in cols]
        for a in range(STEP):
            s = s - cols[a] * y[a]
            w = w - cols[a] * z[a]
    return jnp.concatenate(done, axis=0)


def dot(a, b, dims):
    return lax.dot_general(a, b, (dims, ((), ())), precision=HI, preferred_element_type=F32)


def lower_blocks(n):
    return [(i, j) for i in range(n // SB) for j in range(i + 1)]


def inverse_kernel(packed, out, work, rest):
    n = out.shape[0]
    row_at = lax.broadcasted_iota(jnp.int32, (n, n), 0)
    col_at = lax.broadcasted_iota(jnp.int32, (n, n), 1)
    work[...] = jnp.zeros_like(work)
    for at, (i, j) in enumerate(lower_blocks(n)):
        work[i * SB : (i + 1) * SB, j * SB : (j + 1) * SB] = packed[
            at * SB : (at + 1) * SB, :
        ].astype(F32)
    rest[...] = jnp.where(row_at == col_at, 1.0, 0.0).astype(F32)

    def step(k, _):
        here = pl.ds(pl.multiple_of(k * SB, SB), SB)
        small = invert_block(work[here, here])
        panel = dot(work[:, here], small, ((1,), (1,)))
        below = lax.broadcasted_iota(jnp.int32, (n, SB), 0) >= (k + 1) * SB
        panel = jnp.where(below, panel, 0.0)
        work[...] = work[...] - dot(panel, panel, ((1,), (1,)))
        solved = dot(small, rest[here, :], ((1,), (0,)))
        out[here, :] = solved
        rest[...] = rest[...] - dot(panel, solved, ((1,), (0,)))
        return 0

    lax.fori_loop(0, n // SB, step, 0)


def inverse_factor(packed):
    n = TILE
    vmem = pl.BlockSpec(memory_space=pltpu.VMEM)
    return pl.pallas_call(
        inverse_kernel,
        out_shape=jax.ShapeDtypeStruct((n, n), F32),
        in_specs=[vmem],
        out_specs=vmem,
        scratch_shapes=[pltpu.VMEM((n, n), F32), pltpu.VMEM((n, n), F32)],
        compiler_params=pltpu.CompilerParams(vmem_limit_bytes=24 << 20),
        cost_estimate=pl.CostEstimate(flops=4 * n**3, bytes_accessed=6 * n * n, transcendentals=0),
        name="inverse",
    )(packed)


def pack_kernel(base, out):
    for at, (i, j) in enumerate(lower_blocks(TILE)):
        out[at * SB : (at + 1) * SB, :] = base[0, i * SB : (i + 1) * SB, j * SB : (j + 1) * SB]


def pack_pivot(window):
    rows = len(lower_blocks(TILE)) * SB
    return pl.pallas_call(
        pack_kernel,
        out_shape=jax.ShapeDtypeStruct((rows, SB), window.dtype),
        grid=(1,),
        in_specs=[pl.BlockSpec((1, TILE, TILE), lambda i: (0, 0, 0))],
        out_specs=pl.BlockSpec((rows, SB), lambda i: (0, 0)),
        name="pack",
    )(window)


def swap(block, axis):
    return lax.all_to_all(block, axis, split_axis=0, concat_axis=0, tiled=True)


HOLDERS = 4
QUARTERS = 4


def hand_out(parts, axis, devices):
    mine = jnp.zeros_like(parts[0])
    for part, device in zip(parts, devices):
        if device == 0:
            mine = mine + jnp.where(lax.axis_index(axis) == 0, part, jnp.zeros_like(part))
        else:
            mine = mine + lax.ppermute(part, axis, [(0, device)])
    return mine


def column_holders():
    size = lax.axis_size("col")
    return list(range(0, size, size // HOLDERS))


def to_holders(block):
    parts = list(block.reshape(HOLDERS, -1, block.shape[1]))
    return hand_out(parts, "col", column_holders())


def from_holders(mine):
    size = lax.axis_size("col")
    got = [mine]
    for t in range(1, size):
        got.append(lax.ppermute(mine, "col", [(i, (i - t) % size) for i in column_holders()]))
    return got


def finish_kernel(size, state, *refs):
    halves = refs[:size], refs[size : 2 * size]
    partner, base, added, out, parts, sem = refs[2 * size :]
    column = state[0]
    step = size // HOLDERS
    rows = TILE // HOLDERS
    shift = lax.rem(step - lax.rem(column, step), step)
    first = lax.div(column + shift, step)
    for s in range(step):

        @pl.when(shift == s)
        def _():
            copies = [
                pltpu.make_async_copy(
                    halves[h][k * step + s], parts.at[h, k], sem.at[h * HOLDERS + k]
                )
                for h in range(2)
                for k in range(HOLDERS)
            ]
            for copy in copies:
                copy.start()
            for copy in copies:
                copy.wait()

    for k in range(HOLDERS):
        source = lax.rem(first + k, HOLDERS)
        at = pl.ds(pl.multiple_of(source * rows, rows), rows)
        under = pl.ds(pl.multiple_of(source * rows + TILE, rows), rows)

        @pl.when(column == 0)
        def _():
            out[0, at, :] = parts[0, k]
            out[0, under, :] = parts[1, k]

        @pl.when(column != 0)
        def _():
            def product(part):
                return lax.dot_general(
                    part, partner[...], (((1,), (1,)), ((), ())), preferred_element_type=F32
                )

            upper = base[0, at, :].astype(F32) - state[1].astype(F32) * product(parts[0, k])
            out[0, at, :] = upper.astype(BF16)
            lower = added[at, :] - state[2].astype(F32) * product(parts[1, k])
            out[0, under, :] = lower.astype(BF16)


def finish(state, upper, under, partner, window, added):
    size = len(upper)

    def whole(x):
        return pl.BlockSpec(x.shape, lambda i: (0,) * x.ndim)

    tile = pl.BlockSpec((1, TILE, TILE), lambda i: (0, 0, 0))
    out = jax.ShapeDtypeStruct((1, 2 * TILE, TILE), BF16)
    return pl.pallas_call(
        functools.partial(finish_kernel, size),
        out_shape=out,
        grid=(1,),
        in_specs=[pl.BlockSpec(memory_space=pltpu.SMEM)]
        + [pl.BlockSpec(memory_space=pl.ANY)] * (2 * size)
        + [whole(partner), tile, whole(added)],
        out_specs=whole(out),
        scratch_shapes=[
            pltpu.VMEM((2, HOLDERS, TILE // HOLDERS, TILE), BF16),
            pltpu.SemaphoreType.DMA((2 * HOLDERS,)),
        ],
        compiler_params=pltpu.CompilerParams(vmem_limit_bytes=56 << 20),
        name="finish",
    )(state, *upper, *under, partner, window, added)


def shards(window, children, routes, slots, pattern):
    fronts = lax.axis_size("front")
    rows_axis = lax.axis_size("row")
    columns = lax.axis_size("col")
    front = lax.axis_index("front")
    column = lax.axis_index("col")
    part_rows = TILE // rows_axis
    first = window[0, :TILE]
    packed = pack_pivot(window).reshape(rows_axis, -1, SB)
    share = packed.shape[1]
    pivot_part = swap(packed, "row")[0]
    outgoing, marks = place(routes[:, 0], slots, children, fronts * rows_axis)
    marks = marks.reshape(fronts, rows_axis, CAP)
    near = jnp.where(front == 0, marks[0], marks[1])
    far = jnp.where(front == 0, marks[1], marks[0])
    far = lax.ppermute(far, "front", [(0, 1), (1, 0)])
    both = jnp.concatenate([near, far], axis=1).astype(BF16)[:, None, :]
    both = jnp.pad(both, ((0, 0), (share, 7), (0, SB - both.shape[2])))
    piece = jnp.pad(pivot_part, ((0, 8), (0, 0)))[None]
    row_at = lax.broadcasted_iota(jnp.int32, both.shape, 1)
    arrived = swap(jnp.where(row_at < share, piece, both), "row")
    got = arrived[:, share, : fronts * CAP].astype(jnp.int32).reshape(rows_axis, fronts, CAP)
    near, far = got[:, 0], got[:, 1]
    tags = jnp.stack([jnp.where(front == 0, near, far), jnp.where(front == 0, far, near)])
    tags = tags.reshape(-1)
    pivot = arrived[:, :share].reshape(-1, SB)
    outgoing, tags, pivot = lax.optimization_barrier((outgoing, tags, pivot))
    incoming = swap(outgoing, ("front", "row"))
    inverse = inverse_factor(pivot)

    def solve(rows):
        return lax.dot_general(
            rows.astype(F32), inverse, (((1,), (1,)), ((), ())), precision=HI
        ).astype(BF16)

    def to_plane(lower, odd):
        planes = [c for c in range(1, columns) if c % 2 == odd]
        quarters = lower.reshape(-1, QUARTERS, part_rows, TILE)
        mine = None
        for k in range(QUARTERS):
            pairs = [((c // 2) * columns, k * columns + c) for c in planes]
            got = lax.ppermute(quarters[:, k], ("row", "col"), pairs)
            mine = got if mine is None else mine + got
        return mine

    lower_first = solve(first)
    even = to_plane(lower_first, 0)
    upper = from_holders(to_holders(lower_first))
    incoming, even, upper = lax.optimization_barrier((incoming, even, upper))
    added = assemble(tags, incoming, window)
    lower_second = solve(added)
    odd = to_plane(lower_second, 1)
    piece = jnp.where(column % 2 == 0, even, odd)
    groups = [list(range(k, rows_axis, QUARTERS)) for k in range(QUARTERS)]
    got = lax.all_to_all(
        piece, "row", split_axis=0, concat_axis=0, axis_index_groups=groups, tiled=True
    )
    got, under = lax.optimization_barrier((got, to_holders(lower_second)))
    under = from_holders(under)
    partner = swap(
        jnp.broadcast_to(got[:1], (rows_axis, part_rows, TILE)), "row"
    ).reshape(TILE, TILE)
    state = jnp.concatenate([jnp.full((1,), column, jnp.int32), pattern[0, :, 0]])
    return finish(state, upper, under, partner, window, added)


def solution(mesh):
    placed = (
        P("front", "row", "col"),
        P(("front", "row", "col"), None, None),
        P(("front", "row", "col"), None),
        P(("front", "row", "col")),
        P("front", "row", "col"),
    )
    return jax.shard_map(
        shards, mesh=mesh, in_specs=placed, out_specs=P("front", "row", "col"), check_vma=False
    )
```

```python
import functools

import jax
import jax.numpy as jnp
from jax import lax
from jax.experimental import pallas as pl
from jax.experimental.pallas import tpu as pltpu
from jax.sharding import PartitionSpec as P

TILE = 512
SB = 128
CAP = 2
HI = lax.Precision.HIGHEST
F32 = jnp.float32
BF16 = jnp.bfloat16


def place_kernel(routes, slots, children, outgoing, tags, count, sem):
    n = children.shape[0]
    rows = tags.shape[0]

    def clear_tag(i, _):
        tags[i] = 0
        return 0

    lax.fori_loop(0, rows, clear_tag, 0)

    def clear_count(i, _):
        count[i] = 0
        return 0

    lax.fori_loop(0, count.shape[0], clear_count, 0)

    def send(k, _):
        g = routes[k]
        c = count[g]
        count[g] = c + 1
        at = g * CAP + c
        tags[at] = slots[k] + 1
        pltpu.make_async_copy(children.at[k], outgoing.at[at], sem).start()
        return 0

    lax.fori_loop(0, n, send, 0)
    pltpu.make_async_copy(children, outgoing.at[pl.ds(0, n)], sem).wait()


def place(routes, slots, children, groups):
    rows = groups * CAP
    smem = pl.BlockSpec(memory_space=pltpu.SMEM)
    return pl.pallas_call(
        place_kernel,
        out_shape=(
            jax.ShapeDtypeStruct((rows,) + children.shape[1:], children.dtype),
            jax.ShapeDtypeStruct((rows,), jnp.int32),
        ),
        in_specs=[smem, smem, pl.BlockSpec(memory_space=pltpu.VMEM)],
        out_specs=(pl.BlockSpec(memory_space=pl.ANY), smem),
        scratch_shapes=[pltpu.SMEM((groups,), jnp.int32), pltpu.SemaphoreType.DMA],
        name="place",
    )(routes, slots, children)


def assemble_kernel(tags, incoming, base, out, acc):
    side = TILE // SB
    step = pl.program_id(0)
    blocks = incoming.shape[0]

    @pl.when(step == 0)
    def _():
        acc[...] = jnp.zeros_like(acc)

    def add(s, _):
        t = tags[step * blocks + s]

        @pl.when(t > 0)
        def _():
            acc[t - 1] = acc[t - 1] + incoming[s].astype(F32)

        return 0

    lax.fori_loop(0, blocks, add, 0)

    @pl.when(step == pl.num_programs(0) - 1)
    def _():
        for i in range(side):
            for j in range(side):
                rows, cols = slice(i * SB, (i + 1) * SB), slice(j * SB, (j + 1) * SB)
                out[rows, cols] = base[0, rows, cols].astype(F32) + acc[i * side + j]


def assemble(tags, incoming, window):
    steps = 1
    blocks = incoming.shape[0] // steps
    return pl.pallas_call(
        assemble_kernel,
        out_shape=jax.ShapeDtypeStruct((TILE, TILE), F32),
        grid=(steps,),
        in_specs=[
            pl.BlockSpec(memory_space=pltpu.SMEM),
            pl.BlockSpec((blocks, SB, SB), lambda i: (i, 0, 0)),
            pl.BlockSpec((1, TILE, TILE), lambda i: (0, 1, 0)),
        ],
        out_specs=pl.BlockSpec((TILE, TILE), lambda i: (0, 0)),
        scratch_shapes=[pltpu.VMEM(((TILE // SB) ** 2, SB, SB), F32)],
        compiler_params=pltpu.CompilerParams(vmem_limit_bytes=24 << 20),
        name="assemble",
    )(tags, incoming, window)


STEP = 4


def invert_block(block):
    n = block.shape[0]
    s = block
    row_at = lax.broadcasted_iota(jnp.int32, (n, n), 0)
    col_at = lax.broadcasted_iota(jnp.int32, (n, n), 1)
    w = jnp.where(row_at == col_at, 1.0, 0.0).astype(F32)
    done = []
    top = 0
    for j in range(0, n, STEP):
        local = j - top
        cols = [jnp.broadcast_to(s[:, j + a : j + a + 1], s.shape) for a in range(STEP)]
        r = [s[local + a : local + a + 1, :] for a in range(STEP)]
        v = [w[local + a : local + a + 1, :] for a in range(STEP)]
        p = [[cols[b][local + a : local + a + 1, :] for b in range(STEP)] for a in range(STEP)]
        inv = []
        m = [[None] * STEP for _ in range(STEP)]
        for b in range(STEP):
            inv.append(1.0 / p[b][b])
            for a in range(b + 1, STEP):
                m[a][b] = p[a][b] * inv[b]
                for c in range(b + 1, a + 1):
                    p[a][c] = p[a][c] - m[a][b] * p[c][b]
                r[a] = r[a] - m[a][b] * r[b]
                v[a] = v[a] - m[a][b] * v[b]
        done += [v[a] * lax.rsqrt(p[a][a]) for a in range(STEP)]
        if j + STEP >= n:
            break
        y = [None] * STEP
        z = [None] * STEP
        for a in reversed(range(STEP)):
            y[a] = r[a] * inv[a]
            z[a] = v[a] * inv[a]
            for b in range(a + 1, STEP):
                y[a] = y[a] - m[b][a] * y[b]
                z[a] = z[a] - m[b][a] * z[b]
        skip = (j + STEP) // 8 * 8 - top
        s, w = s[skip:], w[skip:]
        cols = [c[skip:] for c in cols]
        top += skip
        if top < j + STEP:
            keep = lax.broadcasted_iota(jnp.int32, s.shape, 0) >= j + STEP - top
            cols = [jnp.where(keep, c, 0.0) for c in cols]
        for a in range(STEP):
            s = s - cols[a] * y[a]
            w = w - cols[a] * z[a]
    return jnp.concatenate(done, axis=0)


def dot(a, b, dims):
    return lax.dot_general(a, b, (dims, ((), ())), precision=HI, preferred_element_type=F32)


def lower_blocks(n):
    return [(i, j) for i in range(n // SB) for j in range(i + 1)]


def inverse_kernel(packed, out, work, rest):
    n = out.shape[0]
    row_at = lax.broadcasted_iota(jnp.int32, (n, n), 0)
    col_at = lax.broadcasted_iota(jnp.int32, (n, n), 1)
    work[...] = jnp.zeros_like(work)
    for at, (i, j) in enumerate(lower_blocks(n)):
        work[i * SB : (i + 1) * SB, j * SB : (j + 1) * SB] = packed[
            at * SB : (at + 1) * SB, :
        ].astype(F32)
    rest[...] = jnp.where(row_at == col_at, 1.0, 0.0).astype(F32)

    def step(k, _):
        here = pl.ds(pl.multiple_of(k * SB, SB), SB)
        small = invert_block(work[here, here])
        panel = dot(work[:, here], small, ((1,), (1,)))
        below = lax.broadcasted_iota(jnp.int32, (n, SB), 0) >= (k + 1) * SB
        panel = jnp.where(below, panel, 0.0)
        work[...] = work[...] - dot(panel, panel, ((1,), (1,)))
        solved = dot(small, rest[here, :], ((1,), (0,)))
        out[here, :] = solved
        rest[...] = rest[...] - dot(panel, solved, ((1,), (0,)))
        return 0

    lax.fori_loop(0, n // SB, step, 0)


def inverse_factor(packed):
    n = TILE
    vmem = pl.BlockSpec(memory_space=pltpu.VMEM)
    return pl.pallas_call(
        inverse_kernel,
        out_shape=jax.ShapeDtypeStruct((n, n), F32),
        in_specs=[vmem],
        out_specs=vmem,
        scratch_shapes=[pltpu.VMEM((n, n), F32), pltpu.VMEM((n, n), F32)],
        compiler_params=pltpu.CompilerParams(vmem_limit_bytes=24 << 20),
        cost_estimate=pl.CostEstimate(flops=4 * n**3, bytes_accessed=6 * n * n, transcendentals=0),
        name="inverse",
    )(packed)


def pack_kernel(base, out):
    for at, (i, j) in enumerate(lower_blocks(TILE)):
        out[at * SB : (at + 1) * SB, :] = base[0, i * SB : (i + 1) * SB, j * SB : (j + 1) * SB]


def pack_pivot(window):
    rows = len(lower_blocks(TILE)) * SB
    return pl.pallas_call(
        pack_kernel,
        out_shape=jax.ShapeDtypeStruct((rows, SB), window.dtype),
        grid=(1,),
        in_specs=[pl.BlockSpec((1, TILE, TILE), lambda i: (0, 0, 0))],
        out_specs=pl.BlockSpec((rows, SB), lambda i: (0, 0)),
        name="pack",
    )(window)


def swap(block, axis):
    return lax.all_to_all(block, axis, split_axis=0, concat_axis=0, tiled=True)


HOLDERS = 4
QUARTERS = 4


def hand_out(parts, axis, devices):
    mine = jnp.zeros_like(parts[0])
    for part, device in zip(parts, devices):
        if device == 0:
            mine = mine + jnp.where(lax.axis_index(axis) == 0, part, jnp.zeros_like(part))
        else:
            mine = mine + lax.ppermute(part, axis, [(0, device)])
    return mine


def column_holders():
    size = lax.axis_size("col")
    return list(range(0, size, size // HOLDERS))


def to_holders(block):
    parts = list(block.reshape(HOLDERS, -1, block.shape[1]))
    return hand_out(parts, "col", column_holders())


def from_holders(mine):
    size = lax.axis_size("col")
    got = [mine]
    for t in range(1, size):
        got.append(lax.ppermute(mine, "col", [(i, (i - t) % size) for i in column_holders()]))
    return got


def finish_kernel(size, state, *refs):
    halves = refs[:size], refs[size : 2 * size]
    partner_at, window, added_at, out, parts, partner, base, added, sem, rest_sem = refs[2 * size :]
    column = state[0]
    step = size // HOLDERS
    rows = TILE // HOLDERS
    shift = lax.rem(step - lax.rem(column, step), step)
    first = lax.div(column + shift, step)
    others = [
        pltpu.make_async_copy(partner_at, partner, rest_sem.at[0]),
        pltpu.make_async_copy(window.at[0, pl.ds(0, TILE), :], base, rest_sem.at[1]),
        pltpu.make_async_copy(added_at, added, rest_sem.at[2]),
    ]
    for copy in others:
        copy.start()
    for s in range(step):

        @pl.when(shift == s)
        def _():
            copies = [
                pltpu.make_async_copy(
                    halves[h][k * step + s], parts.at[h, k], sem.at[h * HOLDERS + k]
                )
                for h in range(2)
                for k in range(HOLDERS)
            ]
            for copy in copies:
                copy.start()
            for copy in copies:
                copy.wait()

    for copy in others:
        copy.wait()

    for k in range(HOLDERS):
        source = lax.rem(first + k, HOLDERS)
        at = pl.ds(pl.multiple_of(source * rows, rows), rows)
        under = pl.ds(pl.multiple_of(source * rows + TILE, rows), rows)

        @pl.when(column == 0)
        def _():
            out[0, at, :] = parts[0, k]
            out[0, under, :] = parts[1, k]

        @pl.when(column != 0)
        def _():
            def product(part):
                return lax.dot_general(
                    part, partner[...], (((1,), (1,)), ((), ())), preferred_element_type=F32
                )

            upper = base[at, :].astype(F32) - state[1].astype(F32) * product(parts[0, k])
            out[0, at, :] = upper.astype(BF16)
            lower = added[at, :] - state[2].astype(F32) * product(parts[1, k])
            out[0, under, :] = lower.astype(BF16)


def finish(state, upper, under, partner, window, added):
    size = len(upper)
    out = jax.ShapeDtypeStruct((1, 2 * TILE, TILE), BF16)
    return pl.pallas_call(
        functools.partial(finish_kernel, size),
        out_shape=out,
        in_specs=[pl.BlockSpec(memory_space=pltpu.SMEM)]
        + [pl.BlockSpec(memory_space=pl.ANY)] * (2 * size + 3),
        out_specs=pl.BlockSpec(memory_space=pltpu.VMEM),
        scratch_shapes=[
            pltpu.VMEM((2, HOLDERS, TILE // HOLDERS, TILE), BF16),
            pltpu.VMEM((TILE, TILE), BF16),
            pltpu.VMEM((TILE, TILE), BF16),
            pltpu.VMEM((TILE, TILE), F32),
            pltpu.SemaphoreType.DMA((2 * HOLDERS,)),
            pltpu.SemaphoreType.DMA((3,)),
        ],
        compiler_params=pltpu.CompilerParams(vmem_limit_bytes=56 << 20),
        name="finish",
    )(state, *upper, *under, partner, window, added)


def shards(window, children, routes, slots, pattern):
    fronts = lax.axis_size("front")
    rows_axis = lax.axis_size("row")
    columns = lax.axis_size("col")
    front = lax.axis_index("front")
    column = lax.axis_index("col")
    part_rows = TILE // rows_axis
    first = window[0, :TILE]
    packed = pack_pivot(window).reshape(rows_axis, -1, SB)
    share = packed.shape[1]
    pivot_part = swap(packed, "row")[0]
    outgoing, marks = place(routes[:, 0], slots, children, fronts * rows_axis)
    marks = marks.reshape(fronts, rows_axis, CAP)
    near = jnp.where(front == 0, marks[0], marks[1])
    far = jnp.where(front == 0, marks[1], marks[0])
    far = lax.ppermute(far, "front", [(0, 1), (1, 0)])
    both = jnp.concatenate([near, far], axis=1).astype(BF16)[:, None, :]
    both = jnp.pad(both, ((0, 0), (share, 7), (0, SB - both.shape[2])))
    piece = jnp.pad(pivot_part, ((0, 8), (0, 0)))[None]
    row_at = lax.broadcasted_iota(jnp.int32, both.shape, 1)
    arrived = swap(jnp.where(row_at < share, piece, both), "row")
    got = arrived[:, share, : fronts * CAP].astype(jnp.int32).reshape(rows_axis, fronts, CAP)
    near, far = got[:, 0], got[:, 1]
    tags = jnp.stack([jnp.where(front == 0, near, far), jnp.where(front == 0, far, near)])
    tags = tags.reshape(-1)
    pivot = arrived[:, :share].reshape(-1, SB)
    outgoing, tags, pivot = lax.optimization_barrier((outgoing, tags, pivot))
    incoming = swap(outgoing, ("front", "row"))
    inverse = inverse_factor(pivot)

    def solve(rows):
        return lax.dot_general(
            rows.astype(F32), inverse, (((1,), (1,)), ((), ())), precision=HI
        ).astype(BF16)

    def to_plane(lower, odd):
        planes = [c for c in range(1, columns) if c % 2 == odd]
        quarters = lower.reshape(-1, QUARTERS, part_rows, TILE)
        mine = None
        for k in range(QUARTERS):
            pairs = [((c // 2) * columns, k * columns + c) for c in planes]
            got = lax.ppermute(quarters[:, k], ("row", "col"), pairs)
            mine = got if mine is None else mine + got
        return mine

    lower_first = solve(first)
    even = to_plane(lower_first, 0)
    upper = from_holders(to_holders(lower_first))
    incoming, even, upper = lax.optimization_barrier((incoming, even, upper))
    added = assemble(tags, incoming, window)
    lower_second = solve(added)
    odd = to_plane(lower_second, 1)
    piece = jnp.where(column % 2 == 0, even, odd)
    groups = [list(range(k, rows_axis, QUARTERS)) for k in range(QUARTERS)]
    got = lax.all_to_all(
        piece, "row", split_axis=0, concat_axis=0, axis_index_groups=groups, tiled=True
    )
    got, under = lax.optimization_barrier((got, to_holders(lower_second)))
    under = from_holders(under)
    near = [1, columns - 1, 2]
    got, *arrived = lax.optimization_barrier((got, *(under[t] for t in near)))
    for t, part in zip(near, arrived):
        under[t] = part
    partner = swap(
        jnp.broadcast_to(got[:1], (rows_axis, part_rows, TILE)), "row"
    ).reshape(TILE, TILE)
    state = jnp.concatenate([jnp.full((1,), column, jnp.int32), pattern[0, :, 0]])
    return finish(state, upper, under, partner, window, added)


def solution(mesh):
    placed = (
        P("front", "row", "col"),
        P(("front", "row", "col"), None, None),
        P(("front", "row", "col"), None),
        P(("front", "row", "col")),
        P("front", "row", "col"),
    )
    return jax.shard_map(
        shards, mesh=mesh, in_specs=placed, out_specs=P("front", "row", "col"), check_vma=False
    )
```

```python
import functools

import jax
import jax.numpy as jnp
from jax import lax
from jax.experimental import pallas as pl
from jax.experimental.pallas import tpu as pltpu
from jax.sharding import PartitionSpec as P

TILE = 512
SB = 128
CAP = 2
HI = lax.Precision.HIGHEST
F32 = jnp.float32
BF16 = jnp.bfloat16


def place_kernel(routes, slots, children, outgoing, tags, count, sem):
    n = children.shape[0]
    rows = tags.shape[0]

    def clear_tag(i, _):
        tags[i] = 0
        return 0

    lax.fori_loop(0, rows, clear_tag, 0)

    def clear_count(i, _):
        count[i] = 0
        return 0

    lax.fori_loop(0, count.shape[0], clear_count, 0)

    def send(k, _):
        g = routes[k]
        c = count[g]
        count[g] = c + 1
        at = g * CAP + c
        tags[at] = slots[k] + 1
        pltpu.make_async_copy(children.at[k], outgoing.at[at], sem).start()
        return 0

    lax.fori_loop(0, n, send, 0)
    pltpu.make_async_copy(children, outgoing.at[pl.ds(0, n)], sem).wait()


def place(routes, slots, children, groups):
    rows = groups * CAP
    smem = pl.BlockSpec(memory_space=pltpu.SMEM)
    return pl.pallas_call(
        place_kernel,
        out_shape=(
            jax.ShapeDtypeStruct((rows,) + children.shape[1:], children.dtype),
            jax.ShapeDtypeStruct((rows,), jnp.int32),
        ),
        in_specs=[smem, smem, pl.BlockSpec(memory_space=pltpu.VMEM)],
        out_specs=(pl.BlockSpec(memory_space=pl.ANY), smem),
        scratch_shapes=[pltpu.SMEM((groups,), jnp.int32), pltpu.SemaphoreType.DMA],
        name="place",
    )(routes, slots, children)


def assemble_kernel(tags, incoming, window, out, blocks, base, acc, sem):
    side = TILE // SB
    pieces = sem.shape[0] - 1
    size = incoming.shape[0] // pieces
    copies = [
        pltpu.make_async_copy(
            incoming.at[pl.ds(p * size, size)], blocks.at[pl.ds(p * size, size)], sem.at[p]
        )
        for p in range(pieces)
    ]
    copies.append(
        pltpu.make_async_copy(window.at[0, pl.ds(TILE, TILE), :], base, sem.at[pieces])
    )
    for copy in copies:
        copy.start()
    acc[...] = jnp.zeros_like(acc)

    def add(s, _):
        t = tags[s]

        @pl.when(t > 0)
        def _():
            acc[t - 1] = acc[t - 1] + blocks[s].astype(F32)

        return 0

    for p in range(pieces):
        copies[p].wait()
        lax.fori_loop(p * size, (p + 1) * size, add, 0)
    copies[pieces].wait()
    for i in range(side):
        for j in range(side):
            rows, cols = slice(i * SB, (i + 1) * SB), slice(j * SB, (j + 1) * SB)
            out[rows, cols] = base[rows, cols].astype(F32) + acc[i * side + j]


def assemble(tags, incoming, window):
    pieces = 4
    return pl.pallas_call(
        assemble_kernel,
        out_shape=jax.ShapeDtypeStruct((TILE, TILE), F32),
        in_specs=[
            pl.BlockSpec(memory_space=pltpu.SMEM),
            pl.BlockSpec(memory_space=pl.ANY),
            pl.BlockSpec(memory_space=pl.ANY),
        ],
        out_specs=pl.BlockSpec(memory_space=pltpu.VMEM),
        scratch_shapes=[
            pltpu.VMEM(incoming.shape, BF16),
            pltpu.VMEM((TILE, TILE), BF16),
            pltpu.VMEM(((TILE // SB) ** 2, SB, SB), F32),
            pltpu.SemaphoreType.DMA((pieces + 1,)),
        ],
        compiler_params=pltpu.CompilerParams(vmem_limit_bytes=24 << 20),
        name="assemble",
    )(tags, incoming, window)


STEP = 4


def invert_block(block):
    n = block.shape[0]
    s = block
    row_at = lax.broadcasted_iota(jnp.int32, (n, n), 0)
    col_at = lax.broadcasted_iota(jnp.int32, (n, n), 1)
    w = jnp.where(row_at == col_at, 1.0, 0.0).astype(F32)
    done = []
    top = 0
    for j in range(0, n, STEP):
        local = j - top
        cols = [jnp.broadcast_to(s[:, j + a : j + a + 1], s.shape) for a in range(STEP)]
        r = [s[local + a : local + a + 1, :] for a in range(STEP)]
        v = [w[local + a : local + a + 1, :] for a in range(STEP)]
        p = [[cols[b][local + a : local + a + 1, :] for b in range(STEP)] for a in range(STEP)]
        inv = []
        m = [[None] * STEP for _ in range(STEP)]
        for b in range(STEP):
            inv.append(1.0 / p[b][b])
            for a in range(b + 1, STEP):
                m[a][b] = p[a][b] * inv[b]
                for c in range(b + 1, a + 1):
                    p[a][c] = p[a][c] - m[a][b] * p[c][b]
                r[a] = r[a] - m[a][b] * r[b]
                v[a] = v[a] - m[a][b] * v[b]
        done += [v[a] * lax.rsqrt(p[a][a]) for a in range(STEP)]
        if j + STEP >= n:
            break
        y = [None] * STEP
        z = [None] * STEP
        for a in reversed(range(STEP)):
            y[a] = r[a] * inv[a]
            z[a] = v[a] * inv[a]
            for b in range(a + 1, STEP):
                y[a] = y[a] - m[b][a] * y[b]
                z[a] = z[a] - m[b][a] * z[b]
        skip = (j + STEP) // 8 * 8 - top
        s, w = s[skip:], w[skip:]
        cols = [c[skip:] for c in cols]
        top += skip
        if top < j + STEP:
            keep = lax.broadcasted_iota(jnp.int32, s.shape, 0) >= j + STEP - top
            cols = [jnp.where(keep, c, 0.0) for c in cols]
        for a in range(STEP):
            s = s - cols[a] * y[a]
            w = w - cols[a] * z[a]
    return jnp.concatenate(done, axis=0)


def dot(a, b, dims):
    return lax.dot_general(a, b, (dims, ((), ())), precision=HI, preferred_element_type=F32)


def lower_blocks(n):
    return [(i, j) for i in range(n // SB) for j in range(i + 1)]


def inverse_kernel(packed, out, work, rest):
    n = out.shape[0]
    row_at = lax.broadcasted_iota(jnp.int32, (n, n), 0)
    col_at = lax.broadcasted_iota(jnp.int32, (n, n), 1)
    work[...] = jnp.zeros_like(work)
    for at, (i, j) in enumerate(lower_blocks(n)):
        work[i * SB : (i + 1) * SB, j * SB : (j + 1) * SB] = packed[
            at * SB : (at + 1) * SB, :
        ].astype(F32)
    rest[...] = jnp.where(row_at == col_at, 1.0, 0.0).astype(F32)

    def step(k, _):
        here = pl.ds(pl.multiple_of(k * SB, SB), SB)
        small = invert_block(work[here, here])
        panel = dot(work[:, here], small, ((1,), (1,)))
        below = lax.broadcasted_iota(jnp.int32, (n, SB), 0) >= (k + 1) * SB
        panel = jnp.where(below, panel, 0.0)
        work[...] = work[...] - dot(panel, panel, ((1,), (1,)))
        solved = dot(small, rest[here, :], ((1,), (0,)))
        out[here, :] = solved
        rest[...] = rest[...] - dot(panel, solved, ((1,), (0,)))
        return 0

    lax.fori_loop(0, n // SB, step, 0)


def inverse_factor(packed):
    n = TILE
    vmem = pl.BlockSpec(memory_space=pltpu.VMEM)
    return pl.pallas_call(
        inverse_kernel,
        out_shape=jax.ShapeDtypeStruct((n, n), F32),
        in_specs=[vmem],
        out_specs=vmem,
        scratch_shapes=[pltpu.VMEM((n, n), F32), pltpu.VMEM((n, n), F32)],
        compiler_params=pltpu.CompilerParams(vmem_limit_bytes=24 << 20),
        cost_estimate=pl.CostEstimate(flops=4 * n**3, bytes_accessed=6 * n * n, transcendentals=0),
        name="inverse",
    )(packed)


def pack_kernel(base, out):
    for at, (i, j) in enumerate(lower_blocks(TILE)):
        out[at * SB : (at + 1) * SB, :] = base[0, i * SB : (i + 1) * SB, j * SB : (j + 1) * SB]


def pack_pivot(window):
    rows = len(lower_blocks(TILE)) * SB
    return pl.pallas_call(
        pack_kernel,
        out_shape=jax.ShapeDtypeStruct((rows, SB), window.dtype),
        grid=(1,),
        in_specs=[pl.BlockSpec((1, TILE, TILE), lambda i: (0, 0, 0))],
        out_specs=pl.BlockSpec((rows, SB), lambda i: (0, 0)),
        name="pack",
    )(window)


def swap(block, axis):
    return lax.all_to_all(block, axis, split_axis=0, concat_axis=0, tiled=True)


HOLDERS = 4
QUARTERS = 4


def hand_out(parts, axis, devices):
    mine = jnp.zeros_like(parts[0])
    for part, device in zip(parts, devices):
        if device == 0:
            mine = mine + jnp.where(lax.axis_index(axis) == 0, part, jnp.zeros_like(part))
        else:
            mine = mine + lax.ppermute(part, axis, [(0, device)])
    return mine


def column_holders():
    size = lax.axis_size("col")
    return list(range(0, size, size // HOLDERS))


def to_holders(block):
    parts = list(block.reshape(HOLDERS, -1, block.shape[1]))
    return hand_out(parts, "col", column_holders())


def from_holders(mine):
    size = lax.axis_size("col")
    got = [mine]
    for t in range(1, size):
        got.append(lax.ppermute(mine, "col", [(i, (i - t) % size) for i in column_holders()]))
    return got


def finish_kernel(size, state, *refs):
    halves = refs[:size], refs[size : 2 * size]
    partner_at, window, added_at, out, parts, partner, base, added, sem, rest_sem = refs[2 * size :]
    column = state[0]
    step = size // HOLDERS
    rows = TILE // HOLDERS
    shift = lax.rem(step - lax.rem(column, step), step)
    first = lax.div(column + shift, step)
    others = [
        pltpu.make_async_copy(partner_at, partner, rest_sem.at[0]),
        pltpu.make_async_copy(window.at[0, pl.ds(0, TILE), :], base, rest_sem.at[1]),
        pltpu.make_async_copy(added_at, added, rest_sem.at[2]),
    ]
    for copy in others:
        copy.start()
    for s in range(step):

        @pl.when(shift == s)
        def _():
            copies = [
                pltpu.make_async_copy(
                    halves[h][k * step + s], parts.at[h, k], sem.at[h * HOLDERS + k]
                )
                for h in range(2)
                for k in range(HOLDERS)
            ]
            for copy in copies:
                copy.start()
            for copy in copies:
                copy.wait()

    for copy in others:
        copy.wait()

    for k in range(HOLDERS):
        source = lax.rem(first + k, HOLDERS)
        at = pl.ds(pl.multiple_of(source * rows, rows), rows)
        under = pl.ds(pl.multiple_of(source * rows + TILE, rows), rows)

        @pl.when(column == 0)
        def _():
            out[0, at, :] = parts[0, k]
            out[0, under, :] = parts[1, k]

        @pl.when(column != 0)
        def _():
            def product(part):
                return lax.dot_general(
                    part, partner[...], (((1,), (1,)), ((), ())), preferred_element_type=F32
                )

            upper = base[at, :].astype(F32) - state[1].astype(F32) * product(parts[0, k])
            out[0, at, :] = upper.astype(BF16)
            lower = added[at, :] - state[2].astype(F32) * product(parts[1, k])
            out[0, under, :] = lower.astype(BF16)


def finish(state, upper, under, partner, window, added):
    size = len(upper)
    out = jax.ShapeDtypeStruct((1, 2 * TILE, TILE), BF16)
    return pl.pallas_call(
        functools.partial(finish_kernel, size),
        out_shape=out,
        in_specs=[pl.BlockSpec(memory_space=pltpu.SMEM)]
        + [pl.BlockSpec(memory_space=pl.ANY)] * (2 * size + 3),
        out_specs=pl.BlockSpec(memory_space=pltpu.VMEM),
        scratch_shapes=[
            pltpu.VMEM((2, HOLDERS, TILE // HOLDERS, TILE), BF16),
            pltpu.VMEM((TILE, TILE), BF16),
            pltpu.VMEM((TILE, TILE), BF16),
            pltpu.VMEM((TILE, TILE), F32),
            pltpu.SemaphoreType.DMA((2 * HOLDERS,)),
            pltpu.SemaphoreType.DMA((3,)),
        ],
        compiler_params=pltpu.CompilerParams(vmem_limit_bytes=56 << 20),
        name="finish",
    )(state, *upper, *under, partner, window, added)


def shards(window, children, routes, slots, pattern):
    fronts = lax.axis_size("front")
    rows_axis = lax.axis_size("row")
    columns = lax.axis_size("col")
    front = lax.axis_index("front")
    column = lax.axis_index("col")
    part_rows = TILE // rows_axis
    first = window[0, :TILE]
    packed = pack_pivot(window).reshape(rows_axis, -1, SB)
    share = packed.shape[1]
    pivot_part = swap(packed, "row")[0]
    outgoing, marks = place(routes[:, 0], slots, children, fronts * rows_axis)
    marks = marks.reshape(fronts, rows_axis, CAP)
    near = jnp.where(front == 0, marks[0], marks[1])
    far = jnp.where(front == 0, marks[1], marks[0])
    far = lax.ppermute(far, "front", [(0, 1), (1, 0)])
    both = jnp.concatenate([near, far], axis=1).astype(BF16)[:, None, :]
    both = jnp.pad(both, ((0, 0), (share, 7), (0, SB - both.shape[2])))
    piece = jnp.pad(pivot_part, ((0, 8), (0, 0)))[None]
    row_at = lax.broadcasted_iota(jnp.int32, both.shape, 1)
    arrived = swap(jnp.where(row_at < share, piece, both), "row")
    got = arrived[:, share, : fronts * CAP].astype(jnp.int32).reshape(rows_axis, fronts, CAP)
    near, far = got[:, 0], got[:, 1]
    tags = jnp.stack([jnp.where(front == 0, near, far), jnp.where(front == 0, far, near)])
    tags = tags.reshape(-1)
    pivot = arrived[:, :share].reshape(-1, SB)
    outgoing, tags, pivot = lax.optimization_barrier((outgoing, tags, pivot))
    incoming = swap(outgoing, ("front", "row"))
    inverse = inverse_factor(pivot)

    def solve(rows):
        return lax.dot_general(
            rows.astype(F32), inverse, (((1,), (1,)), ((), ())), precision=HI
        ).astype(BF16)

    def to_plane(lower, odd):
        planes = [c for c in range(1, columns) if c % 2 == odd]
        quarters = lower.reshape(-1, QUARTERS, part_rows, TILE)
        mine = None
        for k in range(QUARTERS):
            pairs = [((c // 2) * columns, k * columns + c) for c in planes]
            got = lax.ppermute(quarters[:, k], ("row", "col"), pairs)
            mine = got if mine is None else mine + got
        return mine

    lower_first = solve(first)
    even = to_plane(lower_first, 0)
    upper = from_holders(to_holders(lower_first))
    incoming, even, upper = lax.optimization_barrier((incoming, even, upper))
    added = assemble(tags, incoming, window)
    lower_second = solve(added)
    odd = to_plane(lower_second, 1)
    piece = jnp.where(column % 2 == 0, even, odd)
    groups = [list(range(k, rows_axis, QUARTERS)) for k in range(QUARTERS)]
    got = lax.all_to_all(
        piece, "row", split_axis=0, concat_axis=0, axis_index_groups=groups, tiled=True
    )
    under = from_holders(to_holders(lower_second))
    near = [1, columns - 1]
    got, *arrived = lax.optimization_barrier((got, *(under[t] for t in near)))
    for t, part in zip(near, arrived):
        under[t] = part
    partner = swap(
        jnp.broadcast_to(got[:1], (rows_axis, part_rows, TILE)), "row"
    ).reshape(TILE, TILE)
    state = jnp.concatenate([jnp.full((1,), column, jnp.int32), pattern[0, :, 0]])
    return finish(state, upper, under, partner, window, added)


def solution(mesh):
    placed = (
        P("front", "row", "col"),
        P(("front", "row", "col"), None, None),
        P(("front", "row", "col"), None),
        P(("front", "row", "col")),
        P("front", "row", "col"),
    )
    return jax.shard_map(
        shards, mesh=mesh, in_specs=placed, out_specs=P("front", "row", "col"), check_vma=False
    )
```

```python
import functools

import jax
import jax.numpy as jnp
from jax import lax
from jax.experimental import pallas as pl
from jax.experimental.pallas import tpu as pltpu
from jax.sharding import PartitionSpec as P

TILE = 512
SB = 128
CAP = 2
HI = lax.Precision.HIGHEST
F32 = jnp.float32
BF16 = jnp.bfloat16


def place_kernel(routes, slots, children, outgoing, tags, count, sem):
    n = children.shape[0]
    rows = tags.shape[0]

    def clear_tag(i, _):
        tags[i] = 0
        return 0

    lax.fori_loop(0, rows, clear_tag, 0)

    def clear_count(i, _):
        count[i] = 0
        return 0

    lax.fori_loop(0, count.shape[0], clear_count, 0)

    def send(k, _):
        g = routes[k]
        c = count[g]
        count[g] = c + 1
        at = g * CAP + c
        tags[at] = slots[k] + 1
        pltpu.make_async_copy(children.at[k], outgoing.at[at], sem).start()
        return 0

    lax.fori_loop(0, n, send, 0)
    pltpu.make_async_copy(children, outgoing.at[pl.ds(0, n)], sem).wait()


def place(routes, slots, children, groups):
    rows = groups * CAP
    smem = pl.BlockSpec(memory_space=pltpu.SMEM)
    return pl.pallas_call(
        place_kernel,
        out_shape=(
            jax.ShapeDtypeStruct((rows,) + children.shape[1:], children.dtype),
            jax.ShapeDtypeStruct((rows,), jnp.int32),
        ),
        in_specs=[smem, smem, pl.BlockSpec(memory_space=pltpu.VMEM)],
        out_specs=(pl.BlockSpec(memory_space=pl.ANY), smem),
        scratch_shapes=[pltpu.SMEM((groups,), jnp.int32), pltpu.SemaphoreType.DMA],
        name="place",
    )(routes, slots, children)


def assemble_kernel(tags, incoming, window, out, blocks, base, acc, sem):
    side = TILE // SB
    pieces = sem.shape[0] - 1
    size = incoming.shape[0] // pieces
    copies = [
        pltpu.make_async_copy(
            incoming.at[pl.ds(p * size, size)], blocks.at[pl.ds(p * size, size)], sem.at[p]
        )
        for p in range(pieces)
    ]
    copies.append(
        pltpu.make_async_copy(window.at[0, pl.ds(TILE, TILE), :], base, sem.at[pieces])
    )
    for copy in copies:
        copy.start()
    acc[...] = jnp.zeros_like(acc)

    def add(s, _):
        t = tags[s]

        @pl.when(t > 0)
        def _():
            acc[t - 1] = acc[t - 1] + blocks[s].astype(F32)

        return 0

    for p in range(pieces):
        copies[p].wait()
        lax.fori_loop(p * size, (p + 1) * size, add, 0)
    copies[pieces].wait()
    for i in range(side):
        for j in range(side):
            rows, cols = slice(i * SB, (i + 1) * SB), slice(j * SB, (j + 1) * SB)
            out[rows, cols] = base[rows, cols].astype(F32) + acc[i * side + j]


def assemble(tags, incoming, window):
    pieces = 4
    return pl.pallas_call(
        assemble_kernel,
        out_shape=jax.ShapeDtypeStruct((TILE, TILE), F32),
        in_specs=[
            pl.BlockSpec(memory_space=pltpu.SMEM),
            pl.BlockSpec(memory_space=pl.ANY),
            pl.BlockSpec(memory_space=pl.ANY),
        ],
        out_specs=pl.BlockSpec(memory_space=pltpu.VMEM),
        scratch_shapes=[
            pltpu.VMEM(incoming.shape, BF16),
            pltpu.VMEM((TILE, TILE), BF16),
            pltpu.VMEM(((TILE // SB) ** 2, SB, SB), F32),
            pltpu.SemaphoreType.DMA((pieces + 1,)),
        ],
        compiler_params=pltpu.CompilerParams(vmem_limit_bytes=24 << 20),
        name="assemble",
    )(tags, incoming, window)


STEP = 4


def invert_block(block):
    n = block.shape[0]
    s = block
    row_at = lax.broadcasted_iota(jnp.int32, (n, n), 0)
    col_at = lax.broadcasted_iota(jnp.int32, (n, n), 1)
    w = jnp.where(row_at == col_at, 1.0, 0.0).astype(F32)
    done = []
    top = 0
    for j in range(0, n, STEP):
        local = j - top
        cols = [jnp.broadcast_to(s[:, j + a : j + a + 1], s.shape) for a in range(STEP)]
        r = [s[local + a : local + a + 1, :] for a in range(STEP)]
        v = [w[local + a : local + a + 1, :] for a in range(STEP)]
        p = [[cols[b][local + a : local + a + 1, :] for b in range(STEP)] for a in range(STEP)]
        inv = []
        m = [[None] * STEP for _ in range(STEP)]
        for b in range(STEP):
            inv.append(1.0 / p[b][b])
            for a in range(b + 1, STEP):
                m[a][b] = p[a][b] * inv[b]
                for c in range(b + 1, a + 1):
                    p[a][c] = p[a][c] - m[a][b] * p[c][b]
                r[a] = r[a] - m[a][b] * r[b]
                v[a] = v[a] - m[a][b] * v[b]
        done += [v[a] * lax.rsqrt(p[a][a]) for a in range(STEP)]
        if j + STEP >= n:
            break
        y = [None] * STEP
        z = [None] * STEP
        for a in reversed(range(STEP)):
            y[a] = r[a] * inv[a]
            z[a] = v[a] * inv[a]
            for b in range(a + 1, STEP):
                y[a] = y[a] - m[b][a] * y[b]
                z[a] = z[a] - m[b][a] * z[b]
        skip = (j + STEP) // 8 * 8 - top
        s, w = s[skip:], w[skip:]
        cols = [c[skip:] for c in cols]
        top += skip
        if top < j + STEP:
            keep = lax.broadcasted_iota(jnp.int32, s.shape, 0) >= j + STEP - top
            cols = [jnp.where(keep, c, 0.0) for c in cols]
        for a in range(STEP):
            s = s - cols[a] * y[a]
            w = w - cols[a] * z[a]
    return jnp.concatenate(done, axis=0)


def dot(a, b, dims):
    return lax.dot_general(a, b, (dims, ((), ())), precision=HI, preferred_element_type=F32)


def lower_blocks(n):
    return [(i, j) for i in range(n // SB) for j in range(i + 1)]


def inverse_kernel(packed, out, work, rest):
    n = out.shape[0]
    row_at = lax.broadcasted_iota(jnp.int32, (n, n), 0)
    col_at = lax.broadcasted_iota(jnp.int32, (n, n), 1)
    work[...] = jnp.zeros_like(work)
    for at, (i, j) in enumerate(lower_blocks(n)):
        work[i * SB : (i + 1) * SB, j * SB : (j + 1) * SB] = packed[
            at * SB : (at + 1) * SB, :
        ].astype(F32)
    rest[...] = jnp.where(row_at == col_at, 1.0, 0.0).astype(F32)

    def step(k, _):
        here = pl.ds(pl.multiple_of(k * SB, SB), SB)
        small = invert_block(work[here, here])
        panel = dot(work[:, here], small, ((1,), (1,)))
        below = lax.broadcasted_iota(jnp.int32, (n, SB), 0) >= (k + 1) * SB
        panel = jnp.where(below, panel, 0.0)
        work[...] = work[...] - dot(panel, panel, ((1,), (1,)))
        solved = dot(small, rest[here, :], ((1,), (0,)))
        out[here, :] = solved
        rest[...] = rest[...] - dot(panel, solved, ((1,), (0,)))
        return 0

    lax.fori_loop(0, n // SB, step, 0)


def inverse_factor(packed):
    n = TILE
    vmem = pl.BlockSpec(memory_space=pltpu.VMEM)
    return pl.pallas_call(
        inverse_kernel,
        out_shape=jax.ShapeDtypeStruct((n, n), F32),
        in_specs=[vmem],
        out_specs=vmem,
        scratch_shapes=[pltpu.VMEM((n, n), F32), pltpu.VMEM((n, n), F32)],
        compiler_params=pltpu.CompilerParams(vmem_limit_bytes=24 << 20),
        cost_estimate=pl.CostEstimate(flops=4 * n**3, bytes_accessed=6 * n * n, transcendentals=0),
        name="inverse",
    )(packed)


def pack_kernel(base, out):
    for at, (i, j) in enumerate(lower_blocks(TILE)):
        out[at * SB : (at + 1) * SB, :] = base[0, i * SB : (i + 1) * SB, j * SB : (j + 1) * SB]


def pack_pivot(window):
    rows = len(lower_blocks(TILE)) * SB
    return pl.pallas_call(
        pack_kernel,
        out_shape=jax.ShapeDtypeStruct((rows, SB), window.dtype),
        grid=(1,),
        in_specs=[pl.BlockSpec((1, TILE, TILE), lambda i: (0, 0, 0))],
        out_specs=pl.BlockSpec((rows, SB), lambda i: (0, 0)),
        name="pack",
    )(window)


def swap(block, axis):
    return lax.all_to_all(block, axis, split_axis=0, concat_axis=0, tiled=True)


QUARTERS = 4


def hand_out(parts, axis, devices):
    mine = jnp.zeros_like(parts[0])
    for part, device in zip(parts, devices):
        if device == 0:
            mine = mine + jnp.where(lax.axis_index(axis) == 0, part, jnp.zeros_like(part))
        else:
            mine = mine + lax.ppermute(part, axis, [(0, device)])
    return mine


def to_columns(block):
    size = lax.axis_size("col")
    return hand_out(list(block.reshape(size, -1, block.shape[1])), "col", range(size))


def finish_kernel(
    state, lower_at, first, second, partner_at, window, added_at, out, lower, partner, base, added, sem
):
    column = state[0]

    @pl.when(column == 0)
    def _():
        copies = [
            pltpu.make_async_copy(first, out.at[0, pl.ds(0, TILE), :], sem.at[0]),
            pltpu.make_async_copy(second, out.at[0, pl.ds(TILE, TILE), :], sem.at[1]),
        ]
        for copy in copies:
            copy.start()
        for copy in copies:
            copy.wait()

    @pl.when(column != 0)
    def _():
        copies = [
            pltpu.make_async_copy(lower_at, lower, sem.at[0]),
            pltpu.make_async_copy(partner_at, partner, sem.at[1]),
            pltpu.make_async_copy(window.at[0, pl.ds(0, TILE), :], base, sem.at[2]),
            pltpu.make_async_copy(added_at, added, sem.at[3]),
        ]
        for copy in copies:
            copy.start()
        for copy in copies:
            copy.wait()
        size, both, _ = lower.shape
        rows = both // 2
        for p in range(size):
            product = lax.dot_general(
                lower[p], partner[...], (((1,), (1,)), ((), ())), preferred_element_type=F32
            )
            at = slice(p * rows, (p + 1) * rows)
            under = slice(TILE + p * rows, TILE + (p + 1) * rows)
            upper = base[at, :].astype(F32) - state[1].astype(F32) * product[:rows]
            out[0, at, :] = upper.astype(BF16)
            result = added[at, :] - state[2].astype(F32) * product[rows:]
            out[0, under, :] = result.astype(BF16)


def finish(state, lower, first, second, partner, window, added):
    return pl.pallas_call(
        finish_kernel,
        out_shape=jax.ShapeDtypeStruct((1, 2 * TILE, TILE), BF16),
        in_specs=[pl.BlockSpec(memory_space=pltpu.SMEM)]
        + [pl.BlockSpec(memory_space=pl.ANY)] * 6,
        out_specs=pl.BlockSpec(memory_space=pltpu.VMEM),
        scratch_shapes=[
            pltpu.VMEM(lower.shape, BF16),
            pltpu.VMEM((TILE, TILE), BF16),
            pltpu.VMEM((TILE, TILE), BF16),
            pltpu.VMEM((TILE, TILE), F32),
            pltpu.SemaphoreType.DMA((4,)),
        ],
        compiler_params=pltpu.CompilerParams(vmem_limit_bytes=56 << 20),
        name="finish",
    )(state, lower, first, second, partner, window, added)


def shards(window, children, routes, slots, pattern):
    fronts = lax.axis_size("front")
    rows_axis = lax.axis_size("row")
    columns = lax.axis_size("col")
    front = lax.axis_index("front")
    column = lax.axis_index("col")
    part_rows = TILE // rows_axis
    first = window[0, :TILE]
    packed = pack_pivot(window).reshape(rows_axis, -1, SB)
    share = packed.shape[1]
    pivot_part = swap(packed, "row")[0]
    outgoing, marks = place(routes[:, 0], slots, children, fronts * rows_axis)
    marks = marks.reshape(fronts, rows_axis, CAP)
    near = jnp.where(front == 0, marks[0], marks[1])
    far = jnp.where(front == 0, marks[1], marks[0])
    far = lax.ppermute(far, "front", [(0, 1), (1, 0)])
    both = jnp.concatenate([near, far], axis=1).astype(BF16)[:, None, :]
    both = jnp.pad(both, ((0, 0), (share, 7), (0, SB - both.shape[2])))
    piece = jnp.pad(pivot_part, ((0, 8), (0, 0)))[None]
    row_at = lax.broadcasted_iota(jnp.int32, both.shape, 1)
    arrived = swap(jnp.where(row_at < share, piece, both), "row")
    got = arrived[:, share, : fronts * CAP].astype(jnp.int32).reshape(rows_axis, fronts, CAP)
    near, far = got[:, 0], got[:, 1]
    tags = jnp.stack([jnp.where(front == 0, near, far), jnp.where(front == 0, far, near)])
    tags = tags.reshape(-1)
    pivot = arrived[:, :share].reshape(-1, SB)
    outgoing, tags, pivot = lax.optimization_barrier((outgoing, tags, pivot))
    incoming = swap(outgoing, ("front", "row"))
    inverse = inverse_factor(pivot)

    def solve(rows):
        return lax.dot_general(
            rows.astype(F32), inverse, (((1,), (1,)), ((), ())), precision=HI
        ).astype(BF16)

    def to_plane(lower, odd):
        planes = [c for c in range(1, columns) if c % 2 == odd]
        quarters = lower.reshape(-1, QUARTERS, part_rows, TILE)
        mine = None
        for k in range(QUARTERS):
            pairs = [((c // 2) * columns, k * columns + c) for c in planes]
            got = lax.ppermute(quarters[:, k], ("row", "col"), pairs)
            mine = got if mine is None else mine + got
        return mine

    lower_first = solve(first)
    even = to_plane(lower_first, 0)
    upper = to_columns(lower_first)
    incoming, even, upper = lax.optimization_barrier((incoming, even, upper))
    added = assemble(tags, incoming, window)
    lower_second = solve(added)
    odd = to_plane(lower_second, 1)
    piece = jnp.where(column % 2 == 0, even, odd)
    groups = [list(range(k, rows_axis, QUARTERS)) for k in range(QUARTERS)]
    got = lax.all_to_all(
        piece, "row", split_axis=0, concat_axis=0, axis_index_groups=groups, tiled=True
    )
    under = to_columns(lower_second)
    lower = lax.all_gather(jnp.concatenate([upper, under]), "col", tiled=True)
    lower = lower.reshape(columns, -1, TILE)
    got, under = lax.optimization_barrier((got, under))
    partner = swap(
        jnp.broadcast_to(got[:1], (rows_axis, part_rows, TILE)), "row"
    ).reshape(TILE, TILE)
    state = jnp.concatenate([jnp.full((1,), column, jnp.int32), pattern[0, :, 0]])
    return finish(state, lower, lower_first, lower_second, partner, window, added)


def solution(mesh):
    placed = (
        P("front", "row", "col"),
        P(("front", "row", "col"), None, None),
        P(("front", "row", "col"), None),
        P(("front", "row", "col")),
        P("front", "row", "col"),
    )
    return jax.shard_map(
        shards, mesh=mesh, in_specs=placed, out_specs=P("front", "row", "col"), check_vma=False
    )
```

```python
import functools

import jax
import jax.numpy as jnp
from jax import lax
from jax.experimental import pallas as pl
from jax.experimental.pallas import tpu as pltpu
from jax.sharding import PartitionSpec as P

TILE = 512
SB = 128
CAP = 2
HI = lax.Precision.HIGHEST
F32 = jnp.float32
BF16 = jnp.bfloat16


def place_kernel(routes, slots, children, outgoing, tags, count, sem):
    n = children.shape[0]
    rows = tags.shape[0]

    def clear_tag(i, _):
        tags[i] = 0
        return 0

    lax.fori_loop(0, rows, clear_tag, 0)

    def clear_count(i, _):
        count[i] = 0
        return 0

    lax.fori_loop(0, count.shape[0], clear_count, 0)

    def send(k, _):
        g = routes[k]
        c = count[g]
        count[g] = c + 1
        at = g * CAP + c
        tags[at] = slots[k] + 1
        pltpu.make_async_copy(children.at[k], outgoing.at[at], sem).start()
        return 0

    lax.fori_loop(0, n, send, 0)
    pltpu.make_async_copy(children, outgoing.at[pl.ds(0, n)], sem).wait()


def place(routes, slots, children, groups):
    rows = groups * CAP
    smem = pl.BlockSpec(memory_space=pltpu.SMEM)
    return pl.pallas_call(
        place_kernel,
        out_shape=(
            jax.ShapeDtypeStruct((rows,) + children.shape[1:], children.dtype),
            jax.ShapeDtypeStruct((rows,), jnp.int32),
        ),
        in_specs=[smem, smem, pl.BlockSpec(memory_space=pltpu.VMEM)],
        out_specs=(pl.BlockSpec(memory_space=pl.ANY), smem),
        scratch_shapes=[pltpu.SMEM((groups,), jnp.int32), pltpu.SemaphoreType.DMA],
        name="place",
    )(routes, slots, children)


def assemble_kernel(tags, incoming, window, out, blocks, base, acc, sem):
    side = TILE // SB
    pieces = sem.shape[0] - 1
    size = incoming.shape[0] // pieces
    copies = [
        pltpu.make_async_copy(
            incoming.at[pl.ds(p * size, size)], blocks.at[pl.ds(p * size, size)], sem.at[p]
        )
        for p in range(pieces)
    ]
    copies.append(
        pltpu.make_async_copy(window.at[0, pl.ds(TILE, TILE), :], base, sem.at[pieces])
    )
    for copy in copies:
        copy.start()
    acc[...] = jnp.zeros_like(acc)

    def add(s, _):
        t = tags[s]

        @pl.when(t > 0)
        def _():
            acc[t - 1] = acc[t - 1] + blocks[s].astype(F32)

        return 0

    for p in range(pieces):
        copies[p].wait()
        lax.fori_loop(p * size, (p + 1) * size, add, 0)
    copies[pieces].wait()
    for i in range(side):
        for j in range(side):
            rows, cols = slice(i * SB, (i + 1) * SB), slice(j * SB, (j + 1) * SB)
            out[rows, cols] = base[rows, cols].astype(F32) + acc[i * side + j]


def assemble(tags, incoming, window):
    pieces = 4
    return pl.pallas_call(
        assemble_kernel,
        out_shape=jax.ShapeDtypeStruct((TILE, TILE), F32),
        in_specs=[
            pl.BlockSpec(memory_space=pltpu.SMEM),
            pl.BlockSpec(memory_space=pl.ANY),
            pl.BlockSpec(memory_space=pl.ANY),
        ],
        out_specs=pl.BlockSpec(memory_space=pltpu.VMEM),
        scratch_shapes=[
            pltpu.VMEM(incoming.shape, BF16),
            pltpu.VMEM((TILE, TILE), BF16),
            pltpu.VMEM(((TILE // SB) ** 2, SB, SB), F32),
            pltpu.SemaphoreType.DMA((pieces + 1,)),
        ],
        compiler_params=pltpu.CompilerParams(vmem_limit_bytes=24 << 20),
        name="assemble",
    )(tags, incoming, window)


STEP = 4


def invert_block(block):
    n = block.shape[0]
    s = block
    row_at = lax.broadcasted_iota(jnp.int32, (n, n), 0)
    col_at = lax.broadcasted_iota(jnp.int32, (n, n), 1)
    w = jnp.where(row_at == col_at, 1.0, 0.0).astype(F32)
    done = []
    top = 0
    for j in range(0, n, STEP):
        local = j - top
        cols = [jnp.broadcast_to(s[:, j + a : j + a + 1], s.shape) for a in range(STEP)]
        r = [s[local + a : local + a + 1, :] for a in range(STEP)]
        v = [w[local + a : local + a + 1, :] for a in range(STEP)]
        p = [[cols[b][local + a : local + a + 1, :] for b in range(STEP)] for a in range(STEP)]
        inv = []
        m = [[None] * STEP for _ in range(STEP)]
        for b in range(STEP):
            inv.append(1.0 / p[b][b])
            for a in range(b + 1, STEP):
                m[a][b] = p[a][b] * inv[b]
                for c in range(b + 1, a + 1):
                    p[a][c] = p[a][c] - m[a][b] * p[c][b]
                r[a] = r[a] - m[a][b] * r[b]
                v[a] = v[a] - m[a][b] * v[b]
        done += [v[a] * lax.rsqrt(p[a][a]) for a in range(STEP)]
        if j + STEP >= n:
            break
        y = [None] * STEP
        z = [None] * STEP
        for a in reversed(range(STEP)):
            y[a] = r[a] * inv[a]
            z[a] = v[a] * inv[a]
            for b in range(a + 1, STEP):
                y[a] = y[a] - m[b][a] * y[b]
                z[a] = z[a] - m[b][a] * z[b]
        skip = (j + STEP) // 8 * 8 - top
        s, w = s[skip:], w[skip:]
        cols = [c[skip:] for c in cols]
        top += skip
        if top < j + STEP:
            keep = lax.broadcasted_iota(jnp.int32, s.shape, 0) >= j + STEP - top
            cols = [jnp.where(keep, c, 0.0) for c in cols]
        for a in range(STEP):
            s = s - cols[a] * y[a]
            w = w - cols[a] * z[a]
    return jnp.concatenate(done, axis=0)


def dot(a, b, dims):
    return lax.dot_general(a, b, (dims, ((), ())), precision=HI, preferred_element_type=F32)


def lower_blocks(n):
    return [(i, j) for i in range(n // SB) for j in range(i + 1)]


def inverse_kernel(packed, out, work, rest):
    n = out.shape[0]
    row_at = lax.broadcasted_iota(jnp.int32, (n, n), 0)
    col_at = lax.broadcasted_iota(jnp.int32, (n, n), 1)
    work[...] = jnp.zeros_like(work)
    for at, (i, j) in enumerate(lower_blocks(n)):
        work[i * SB : (i + 1) * SB, j * SB : (j + 1) * SB] = packed[
            at * SB : (at + 1) * SB, :
        ].astype(F32)
    rest[...] = jnp.where(row_at == col_at, 1.0, 0.0).astype(F32)

    def step(k, _):
        here = pl.ds(pl.multiple_of(k * SB, SB), SB)
        small = invert_block(work[here, here])
        panel = dot(work[:, here], small, ((1,), (1,)))
        below = lax.broadcasted_iota(jnp.int32, (n, SB), 0) >= (k + 1) * SB
        panel = jnp.where(below, panel, 0.0)
        work[...] = work[...] - dot(panel, panel, ((1,), (1,)))
        solved = dot(small, rest[here, :], ((1,), (0,)))
        out[here, :] = solved
        rest[...] = rest[...] - dot(panel, solved, ((1,), (0,)))
        return 0

    lax.fori_loop(0, n // SB, step, 0)


def inverse_factor(packed):
    n = TILE
    vmem = pl.BlockSpec(memory_space=pltpu.VMEM)
    return pl.pallas_call(
        inverse_kernel,
        out_shape=jax.ShapeDtypeStruct((n, n), F32),
        in_specs=[vmem],
        out_specs=vmem,
        scratch_shapes=[pltpu.VMEM((n, n), F32), pltpu.VMEM((n, n), F32)],
        compiler_params=pltpu.CompilerParams(vmem_limit_bytes=24 << 20),
        cost_estimate=pl.CostEstimate(flops=4 * n**3, bytes_accessed=6 * n * n, transcendentals=0),
        name="inverse",
    )(packed)


def pack_kernel(base, out):
    for at, (i, j) in enumerate(lower_blocks(TILE)):
        out[at * SB : (at + 1) * SB, :] = base[0, i * SB : (i + 1) * SB, j * SB : (j + 1) * SB]


def pack_pivot(window):
    rows = len(lower_blocks(TILE)) * SB
    return pl.pallas_call(
        pack_kernel,
        out_shape=jax.ShapeDtypeStruct((rows, SB), window.dtype),
        grid=(1,),
        in_specs=[pl.BlockSpec((1, TILE, TILE), lambda i: (0, 0, 0))],
        out_specs=pl.BlockSpec((rows, SB), lambda i: (0, 0)),
        name="pack",
    )(window)


def swap(block, axis):
    return lax.all_to_all(block, axis, split_axis=0, concat_axis=0, tiled=True)


HOLDERS = 4
QUARTERS = 4


def hand_out(parts, axis, devices):
    mine = jnp.zeros_like(parts[0])
    for part, device in zip(parts, devices):
        if device == 0:
            mine = mine + jnp.where(lax.axis_index(axis) == 0, part, jnp.zeros_like(part))
        else:
            mine = mine + lax.ppermute(part, axis, [(0, device)])
    return mine


def column_holders():
    size = lax.axis_size("col")
    return list(range(0, size, size // HOLDERS))


def to_holders(block):
    parts = list(block.reshape(HOLDERS, -1, block.shape[1]))
    return hand_out(parts, "col", column_holders())


def from_holders(mine):
    size = lax.axis_size("col")
    got = [mine]
    for t in range(1, size):
        got.append(lax.ppermute(mine, "col", [(i, (i - t) % size) for i in column_holders()]))
    return got


def finish_kernel(size, state, *refs):
    halves = refs[:size], refs[size : 2 * size]
    own = refs[2 * size : 2 * size + 2]
    rest = refs[2 * size + 2 :]
    partner_at, window, added_at, out, parts, partner, base, added, sem, rest_sem = rest
    column = state[0]
    step = size // HOLDERS
    rows = TILE // HOLDERS
    shift = lax.rem(step - lax.rem(column, step), step)
    first = lax.div(column + shift, step)

    @pl.when(column == 0)
    def _():
        copies = [
            pltpu.make_async_copy(
                own[h], out.at[0, pl.ds(h * TILE, TILE), :], rest_sem.at[h]
            )
            for h in range(2)
        ]
        for copy in copies:
            copy.start()
        for copy in copies:
            copy.wait()

    @pl.when(column != 0)
    def _():
        others = [
            pltpu.make_async_copy(partner_at, partner, rest_sem.at[0]),
            pltpu.make_async_copy(window.at[0, pl.ds(0, TILE), :], base, rest_sem.at[1]),
            pltpu.make_async_copy(added_at, added, rest_sem.at[2]),
        ]
        for copy in others:
            copy.start()
        for s in range(step):

            @pl.when(shift == s)
            def _():
                copies = [
                    pltpu.make_async_copy(
                        halves[h][k * step + s], parts.at[h, k], sem.at[h * HOLDERS + k]
                    )
                    for h in range(2)
                    for k in range(HOLDERS)
                ]
                for copy in copies:
                    copy.start()
                for copy in copies:
                    copy.wait()

        for copy in others:
            copy.wait()

        for k in range(HOLDERS):
            source = lax.rem(first + k, HOLDERS)
            at = pl.ds(pl.multiple_of(source * rows, rows), rows)
            under = pl.ds(pl.multiple_of(source * rows + TILE, rows), rows)

            def product(part):
                return lax.dot_general(
                    part, partner[...], (((1,), (1,)), ((), ())), preferred_element_type=F32
                )

            upper = base[at, :].astype(F32) - state[1].astype(F32) * product(parts[0, k])
            out[0, at, :] = upper.astype(BF16)
            lower = added[at, :] - state[2].astype(F32) * product(parts[1, k])
            out[0, under, :] = lower.astype(BF16)


def finish(state, upper, under, own, partner, window, added):
    size = len(upper)
    out = jax.ShapeDtypeStruct((1, 2 * TILE, TILE), BF16)
    return pl.pallas_call(
        functools.partial(finish_kernel, size),
        out_shape=out,
        in_specs=[pl.BlockSpec(memory_space=pltpu.SMEM)]
        + [pl.BlockSpec(memory_space=pl.ANY)] * (2 * size + 5),
        out_specs=pl.BlockSpec(memory_space=pltpu.VMEM),
        scratch_shapes=[
            pltpu.VMEM((2, HOLDERS, TILE // HOLDERS, TILE), BF16),
            pltpu.VMEM((TILE, TILE), BF16),
            pltpu.VMEM((TILE, TILE), BF16),
            pltpu.VMEM((TILE, TILE), F32),
            pltpu.SemaphoreType.DMA((2 * HOLDERS,)),
            pltpu.SemaphoreType.DMA((3,)),
        ],
        compiler_params=pltpu.CompilerParams(vmem_limit_bytes=56 << 20),
        name="finish",
    )(state, *upper, *under, *own, partner, window, added)


def shards(window, children, routes, slots, pattern):
    fronts = lax.axis_size("front")
    rows_axis = lax.axis_size("row")
    columns = lax.axis_size("col")
    front = lax.axis_index("front")
    column = lax.axis_index("col")
    part_rows = TILE // rows_axis
    first = window[0, :TILE]
    packed = pack_pivot(window).reshape(rows_axis, -1, SB)
    share = packed.shape[1]
    pivot_part = swap(packed, "row")[0]
    outgoing, marks = place(routes[:, 0], slots, children, fronts * rows_axis)
    marks = marks.reshape(fronts, rows_axis, CAP)
    near = jnp.where(front == 0, marks[0], marks[1])
    far = jnp.where(front == 0, marks[1], marks[0])
    far = lax.ppermute(far, "front", [(0, 1), (1, 0)])
    both = jnp.concatenate([near, far], axis=1).astype(BF16)[:, None, :]
    both = jnp.pad(both, ((0, 0), (share, 7), (0, SB - both.shape[2])))
    piece = jnp.pad(pivot_part, ((0, 8), (0, 0)))[None]
    row_at = lax.broadcasted_iota(jnp.int32, both.shape, 1)
    arrived = swap(jnp.where(row_at < share, piece, both), "row")
    got = arrived[:, share, : fronts * CAP].astype(jnp.int32).reshape(rows_axis, fronts, CAP)
    near, far = got[:, 0], got[:, 1]
    tags = jnp.stack([jnp.where(front == 0, near, far), jnp.where(front == 0, far, near)])
    tags = tags.reshape(-1)
    pivot = arrived[:, :share].reshape(-1, SB)
    outgoing, tags, pivot = lax.optimization_barrier((outgoing, tags, pivot))
    incoming = swap(outgoing, ("front", "row"))
    inverse = inverse_factor(pivot)

    def solve(rows):
        return lax.dot_general(
            rows.astype(F32), inverse, (((1,), (1,)), ((), ())), precision=HI
        ).astype(BF16)

    def to_plane(lower, odd):
        planes = [c for c in range(1, columns) if c % 2 == odd]
        quarters = lower.reshape(-1, QUARTERS, part_rows, TILE)
        mine = None
        for k in range(QUARTERS):
            pairs = [((c // 2) * columns, k * columns + c) for c in planes]
            got = lax.ppermute(quarters[:, k], ("row", "col"), pairs)
            mine = got if mine is None else mine + got
        return mine

    lower_first = solve(first)
    even = to_plane(lower_first, 0)
    upper = from_holders(to_holders(lower_first))
    incoming, even, upper = lax.optimization_barrier((incoming, even, upper))
    added = assemble(tags, incoming, window)
    lower_second = solve(added)
    odd = to_plane(lower_second, 1)
    piece = jnp.where(column % 2 == 0, even, odd)
    groups = [list(range(k, rows_axis, QUARTERS)) for k in range(QUARTERS)]
    got = lax.all_to_all(
        piece, "row", split_axis=0, concat_axis=0, axis_index_groups=groups, tiled=True
    )
    under = from_holders(to_holders(lower_second))
    near = [1, columns - 1, 2, columns - 2]
    got, *arrived = lax.optimization_barrier((got, *(under[t] for t in near)))
    for t, part in zip(near, arrived):
        under[t] = part
    partner = swap(
        jnp.broadcast_to(got[:1], (rows_axis, part_rows, TILE)), "row"
    ).reshape(TILE, TILE)
    state = jnp.concatenate([jnp.full((1,), column, jnp.int32), pattern[0, :, 0]])
    return finish(state, upper, under, (lower_first, lower_second), partner, window, added)


def solution(mesh):
    placed = (
        P("front", "row", "col"),
        P(("front", "row", "col"), None, None),
        P(("front", "row", "col"), None),
        P(("front", "row", "col")),
        P("front", "row", "col"),
    )
    return jax.shard_map(
        shards, mesh=mesh, in_specs=placed, out_specs=P("front", "row", "col"), check_vma=False
    )
```

```python
import functools

import jax
import jax.numpy as jnp
from jax import lax
from jax.experimental import pallas as pl
from jax.experimental.pallas import tpu as pltpu
from jax.sharding import PartitionSpec as P

TILE = 512
SB = 128
CAP = 2
HI = lax.Precision.HIGHEST
F32 = jnp.float32
BF16 = jnp.bfloat16


def place_kernel(routes, slots, children, outgoing, tags, count, sem):
    n = children.shape[0]
    rows = tags.shape[0]

    def clear_tag(i, _):
        tags[i] = 0
        return 0

    lax.fori_loop(0, rows, clear_tag, 0)

    def clear_count(i, _):
        count[i] = 0
        return 0

    lax.fori_loop(0, count.shape[0], clear_count, 0)

    def send(k, _):
        g = routes[k]
        c = count[g]
        count[g] = c + 1
        at = g * CAP + c
        tags[at] = slots[k] + 1
        pltpu.make_async_copy(children.at[k], outgoing.at[at], sem).start()
        return 0

    lax.fori_loop(0, n, send, 0)
    pltpu.make_async_copy(children, outgoing.at[pl.ds(0, n)], sem).wait()


def place(routes, slots, children, groups):
    rows = groups * CAP
    smem = pl.BlockSpec(memory_space=pltpu.SMEM)
    return pl.pallas_call(
        place_kernel,
        out_shape=(
            jax.ShapeDtypeStruct((rows,) + children.shape[1:], children.dtype),
            jax.ShapeDtypeStruct((rows,), jnp.int32),
        ),
        in_specs=[smem, smem, pl.BlockSpec(memory_space=pltpu.VMEM)],
        out_specs=(pl.BlockSpec(memory_space=pl.ANY), smem),
        scratch_shapes=[pltpu.SMEM((groups,), jnp.int32), pltpu.SemaphoreType.DMA],
        name="place",
    )(routes, slots, children)


def assemble_kernel(tags, incoming, window, out, blocks, base, acc, sem):
    side = TILE // SB
    pieces = sem.shape[0] - 1
    size = incoming.shape[0] // pieces
    copies = [
        pltpu.make_async_copy(
            incoming.at[pl.ds(p * size, size)], blocks.at[pl.ds(p * size, size)], sem.at[p]
        )
        for p in range(pieces)
    ]
    copies.append(
        pltpu.make_async_copy(window.at[0, pl.ds(TILE, TILE), :], base, sem.at[pieces])
    )
    for copy in copies:
        copy.start()
    acc[...] = jnp.zeros_like(acc)

    def add(s, _):
        t = tags[s]

        @pl.when(t > 0)
        def _():
            acc[t - 1] = acc[t - 1] + blocks[s].astype(F32)

        return 0

    for p in range(pieces):
        copies[p].wait()
        lax.fori_loop(p * size, (p + 1) * size, add, 0)
    copies[pieces].wait()
    for i in range(side):
        for j in range(side):
            rows, cols = slice(i * SB, (i + 1) * SB), slice(j * SB, (j + 1) * SB)
            out[rows, cols] = base[rows, cols].astype(F32) + acc[i * side + j]


def assemble(tags, incoming, window):
    pieces = 4
    return pl.pallas_call(
        assemble_kernel,
        out_shape=jax.ShapeDtypeStruct((TILE, TILE), F32),
        in_specs=[
            pl.BlockSpec(memory_space=pltpu.SMEM),
            pl.BlockSpec(memory_space=pl.ANY),
            pl.BlockSpec(memory_space=pl.ANY),
        ],
        out_specs=pl.BlockSpec(memory_space=pltpu.VMEM),
        scratch_shapes=[
            pltpu.VMEM(incoming.shape, BF16),
            pltpu.VMEM((TILE, TILE), BF16),
            pltpu.VMEM(((TILE // SB) ** 2, SB, SB), F32),
            pltpu.SemaphoreType.DMA((pieces + 1,)),
        ],
        compiler_params=pltpu.CompilerParams(vmem_limit_bytes=24 << 20),
        name="assemble",
    )(tags, incoming, window)


STEP = 4


def invert_block(block):
    n = block.shape[0]
    s = block
    row_at = lax.broadcasted_iota(jnp.int32, (n, n), 0)
    col_at = lax.broadcasted_iota(jnp.int32, (n, n), 1)
    w = jnp.where(row_at == col_at, 1.0, 0.0).astype(F32)
    done = []
    top = 0
    for j in range(0, n, STEP):
        local = j - top
        cols = [jnp.broadcast_to(s[:, j + a : j + a + 1], s.shape) for a in range(STEP)]
        r = [s[local + a : local + a + 1, :] for a in range(STEP)]
        v = [w[local + a : local + a + 1, :] for a in range(STEP)]
        p = [[cols[b][local + a : local + a + 1, :] for b in range(STEP)] for a in range(STEP)]
        inv = []
        m = [[None] * STEP for _ in range(STEP)]
        for b in range(STEP):
            inv.append(1.0 / p[b][b])
            for a in range(b + 1, STEP):
                m[a][b] = p[a][b] * inv[b]
                for c in range(b + 1, a + 1):
                    p[a][c] = p[a][c] - m[a][b] * p[c][b]
                r[a] = r[a] - m[a][b] * r[b]
                v[a] = v[a] - m[a][b] * v[b]
        done += [v[a] * lax.rsqrt(p[a][a]) for a in range(STEP)]
        if j + STEP >= n:
            break
        y = [None] * STEP
        z = [None] * STEP
        for a in reversed(range(STEP)):
            y[a] = r[a] * inv[a]
            z[a] = v[a] * inv[a]
            for b in range(a + 1, STEP):
                y[a] = y[a] - m[b][a] * y[b]
                z[a] = z[a] - m[b][a] * z[b]
        skip = (j + STEP) // 8 * 8 - top
        s, w = s[skip:], w[skip:]
        cols = [c[skip:] for c in cols]
        top += skip
        if top < j + STEP:
            keep = lax.broadcasted_iota(jnp.int32, s.shape, 0) >= j + STEP - top
            cols = [jnp.where(keep, c, 0.0) for c in cols]
        for a in range(STEP):
            s = s - cols[a] * y[a]
            w = w - cols[a] * z[a]
    return jnp.concatenate(done, axis=0)


def dot(a, b, dims):
    return lax.dot_general(a, b, (dims, ((), ())), precision=HI, preferred_element_type=F32)


def lower_blocks(n):
    return [(i, j) for i in range(n // SB) for j in range(i + 1)]


def inverse_kernel(packed, out, work, rest):
    n = out.shape[0]
    row_at = lax.broadcasted_iota(jnp.int32, (n, n), 0)
    col_at = lax.broadcasted_iota(jnp.int32, (n, n), 1)
    work[...] = jnp.zeros_like(work)
    for at, (i, j) in enumerate(lower_blocks(n)):
        work[i * SB : (i + 1) * SB, j * SB : (j + 1) * SB] = packed[
            at * SB : (at + 1) * SB, :
        ].astype(F32)
    rest[...] = jnp.where(row_at == col_at, 1.0, 0.0).astype(F32)

    def step(k, _):
        here = pl.ds(pl.multiple_of(k * SB, SB), SB)
        small = invert_block(work[here, here])
        panel = dot(work[:, here], small, ((1,), (1,)))
        below = lax.broadcasted_iota(jnp.int32, (n, SB), 0) >= (k + 1) * SB
        panel = jnp.where(below, panel, 0.0)
        work[...] = work[...] - dot(panel, panel, ((1,), (1,)))
        solved = dot(small, rest[here, :], ((1,), (0,)))
        out[here, :] = solved
        rest[...] = rest[...] - dot(panel, solved, ((1,), (0,)))
        return 0

    lax.fori_loop(0, n // SB, step, 0)


def inverse_factor(packed):
    n = TILE
    vmem = pl.BlockSpec(memory_space=pltpu.VMEM)
    return pl.pallas_call(
        inverse_kernel,
        out_shape=jax.ShapeDtypeStruct((n, n), F32),
        in_specs=[vmem],
        out_specs=vmem,
        scratch_shapes=[pltpu.VMEM((n, n), F32), pltpu.VMEM((n, n), F32)],
        compiler_params=pltpu.CompilerParams(vmem_limit_bytes=24 << 20),
        cost_estimate=pl.CostEstimate(flops=4 * n**3, bytes_accessed=6 * n * n, transcendentals=0),
        name="inverse",
    )(packed)


def pack_kernel(base, out):
    for at, (i, j) in enumerate(lower_blocks(TILE)):
        out[at * SB : (at + 1) * SB, :] = base[0, i * SB : (i + 1) * SB, j * SB : (j + 1) * SB]


def pack_pivot(window):
    rows = len(lower_blocks(TILE)) * SB
    return pl.pallas_call(
        pack_kernel,
        out_shape=jax.ShapeDtypeStruct((rows, SB), window.dtype),
        grid=(1,),
        in_specs=[pl.BlockSpec((1, TILE, TILE), lambda i: (0, 0, 0))],
        out_specs=pl.BlockSpec((rows, SB), lambda i: (0, 0)),
        name="pack",
    )(window)


def swap(block, axis):
    return lax.all_to_all(block, axis, split_axis=0, concat_axis=0, tiled=True)


HOLDERS = 4
QUARTERS = 4


def hand_out(parts, axis, devices):
    mine = jnp.zeros_like(parts[0])
    for part, device in zip(parts, devices):
        if device == 0:
            mine = mine + jnp.where(lax.axis_index(axis) == 0, part, jnp.zeros_like(part))
        else:
            mine = mine + lax.ppermute(part, axis, [(0, device)])
    return mine


def column_holders():
    size = lax.axis_size("col")
    return list(range(0, size, size // HOLDERS))


def to_holders(block):
    parts = list(block.reshape(HOLDERS, -1, block.shape[1]))
    return hand_out(parts, "col", column_holders())


def from_holders(mine):
    size = lax.axis_size("col")
    got = [mine]
    for t in range(1, size):
        pairs = [(i, (i - t) % size) for i in column_holders() if (i - t) % size]
        got.append(lax.ppermute(mine, "col", pairs))
    return got


def finish_kernel(size, state, *refs):
    halves = refs[:size], refs[size : 2 * size]
    own = refs[2 * size : 2 * size + 2]
    rest = refs[2 * size + 2 :]
    partner_at, window, added_at, out, parts, partner, base, added, sem, rest_sem = rest
    column = state[0]
    step = size // HOLDERS
    rows = TILE // HOLDERS
    shift = lax.rem(step - lax.rem(column, step), step)
    first = lax.div(column + shift, step)

    @pl.when(column == 0)
    def _():
        copies = [
            pltpu.make_async_copy(
                own[h], out.at[0, pl.ds(h * TILE, TILE), :], rest_sem.at[h]
            )
            for h in range(2)
        ]
        for copy in copies:
            copy.start()
        for copy in copies:
            copy.wait()

    @pl.when(column != 0)
    def _():
        others = [
            pltpu.make_async_copy(partner_at, partner, rest_sem.at[0]),
            pltpu.make_async_copy(window.at[0, pl.ds(0, TILE), :], base, rest_sem.at[1]),
            pltpu.make_async_copy(added_at, added, rest_sem.at[2]),
        ]
        for copy in others:
            copy.start()
        for s in range(step):

            @pl.when(shift == s)
            def _():
                copies = [
                    pltpu.make_async_copy(
                        halves[h][k * step + s], parts.at[h, k], sem.at[h * HOLDERS + k]
                    )
                    for h in range(2)
                    for k in range(HOLDERS)
                ]
                for copy in copies:
                    copy.start()
                for copy in copies:
                    copy.wait()

        for copy in others:
            copy.wait()

        for k in range(HOLDERS):
            source = lax.rem(first + k, HOLDERS)
            at = pl.ds(pl.multiple_of(source * rows, rows), rows)
            under = pl.ds(pl.multiple_of(source * rows + TILE, rows), rows)

            def product(part):
                return lax.dot_general(
                    part, partner[...], (((1,), (1,)), ((), ())), preferred_element_type=F32
                )

            upper = base[at, :].astype(F32) - state[1].astype(F32) * product(parts[0, k])
            out[0, at, :] = upper.astype(BF16)
            lower = added[at, :] - state[2].astype(F32) * product(parts[1, k])
            out[0, under, :] = lower.astype(BF16)


def finish(state, upper, under, own, partner, window, added):
    size = len(upper)
    out = jax.ShapeDtypeStruct((1, 2 * TILE, TILE), BF16)
    return pl.pallas_call(
        functools.partial(finish_kernel, size),
        out_shape=out,
        in_specs=[pl.BlockSpec(memory_space=pltpu.SMEM)]
        + [pl.BlockSpec(memory_space=pl.ANY)] * (2 * size + 5),
        out_specs=pl.BlockSpec(memory_space=pltpu.VMEM),
        scratch_shapes=[
            pltpu.VMEM((2, HOLDERS, TILE // HOLDERS, TILE), BF16),
            pltpu.VMEM((TILE, TILE), BF16),
            pltpu.VMEM((TILE, TILE), BF16),
            pltpu.VMEM((TILE, TILE), F32),
            pltpu.SemaphoreType.DMA((2 * HOLDERS,)),
            pltpu.SemaphoreType.DMA((3,)),
        ],
        compiler_params=pltpu.CompilerParams(vmem_limit_bytes=56 << 20),
        name="finish",
    )(state, *upper, *under, *own, partner, window, added)


def shards(window, children, routes, slots, pattern):
    fronts = lax.axis_size("front")
    rows_axis = lax.axis_size("row")
    columns = lax.axis_size("col")
    front = lax.axis_index("front")
    column = lax.axis_index("col")
    part_rows = TILE // rows_axis
    first = window[0, :TILE]
    packed = pack_pivot(window).reshape(rows_axis, -1, SB)
    share = packed.shape[1]
    pivot_part = swap(packed, "row")[0]
    outgoing, marks = place(routes[:, 0], slots, children, fronts * rows_axis)
    marks = marks.reshape(fronts, rows_axis, CAP)
    near = jnp.where(front == 0, marks[0], marks[1])
    far = jnp.where(front == 0, marks[1], marks[0])
    far = lax.ppermute(far, "front", [(0, 1), (1, 0)])
    both = jnp.concatenate([near, far], axis=1).astype(BF16)[:, None, :]
    both = jnp.pad(both, ((0, 0), (share, 7), (0, SB - both.shape[2])))
    piece = jnp.pad(pivot_part, ((0, 8), (0, 0)))[None]
    row_at = lax.broadcasted_iota(jnp.int32, both.shape, 1)
    arrived = swap(jnp.where(row_at < share, piece, both), "row")
    got = arrived[:, share, : fronts * CAP].astype(jnp.int32).reshape(rows_axis, fronts, CAP)
    near, far = got[:, 0], got[:, 1]
    tags = jnp.stack([jnp.where(front == 0, near, far), jnp.where(front == 0, far, near)])
    tags = tags.reshape(-1)
    pivot = arrived[:, :share].reshape(-1, SB)
    outgoing, tags, pivot = lax.optimization_barrier((outgoing, tags, pivot))
    incoming = swap(outgoing, ("front", "row"))
    inverse = inverse_factor(pivot)

    def solve(rows):
        return lax.dot_general(
            rows.astype(F32), inverse, (((1,), (1,)), ((), ())), precision=HI
        ).astype(BF16)

    def to_plane(lower, odd):
        planes = [c for c in range(1, columns) if c % 2 == odd]
        quarters = lower.reshape(-1, QUARTERS, part_rows, TILE)
        mine = None
        for k in range(QUARTERS):
            pairs = [((c // 2) * columns, k * columns + c) for c in planes]
            got = lax.ppermute(quarters[:, k], ("row", "col"), pairs)
            mine = got if mine is None else mine + got
        return mine

    lower_first = solve(first)
    even = to_plane(lower_first, 0)
    upper = from_holders(to_holders(lower_first))
    incoming, even, upper = lax.optimization_barrier((incoming, even, upper))
    added = assemble(tags, incoming, window)
    lower_second = solve(added)
    odd = to_plane(lower_second, 1)
    piece = jnp.where(column % 2 == 0, even, odd)
    groups = [list(range(k, rows_axis, QUARTERS)) for k in range(QUARTERS)]
    got = lax.all_to_all(
        piece, "row", split_axis=0, concat_axis=0, axis_index_groups=groups, tiled=True
    )
    under = from_holders(to_holders(lower_second))
    near = [columns // 2, columns // 2 - 1]
    got, *arrived = lax.optimization_barrier((got, *(under[t] for t in near)))
    for t, part in zip(near, arrived):
        under[t] = part
    partner = swap(
        jnp.broadcast_to(got[:1], (rows_axis, part_rows, TILE)), "row"
    ).reshape(TILE, TILE)
    state = jnp.concatenate([jnp.full((1,), column, jnp.int32), pattern[0, :, 0]])
    return finish(state, upper, under, (lower_first, lower_second), partner, window, added)


def solution(mesh):
    placed = (
        P("front", "row", "col"),
        P(("front", "row", "col"), None, None),
        P(("front", "row", "col"), None),
        P(("front", "row", "col")),
        P("front", "row", "col"),
    )
    return jax.shard_map(
        shards, mesh=mesh, in_specs=placed, out_specs=P("front", "row", "col"), check_vma=False
    )
```
